128 devices in a mesh: dom: 128 (over x, z, y, core).
Axes of the slice: x: 4, y: 4, z: 4, core: 2. Of those that a mesh axis runs over, the one named last changes fastest.
Arguments:
- rhs_fields: float32 [64, 524288], P(None, 'dom')
- diag_blocks: float32 [4096, 128, 128], P('dom')
- off_blocks: float32 [4096, 3, 128, 128], P('dom')
- block_cols: int32 [4096, 3], P('dom'), may hold values from 0 to 39, as said below
- send_lists: int32 [128, 2, 4], P('dom'), may hold values from 0 to 31, as said below
- fine_agg: int32 [524288], P('dom'), may hold values from 0 to 127, as said below
- coarse_diag: float32 [128, 128, 128], P('dom')
- coarse_side: float32 [128, 2, 128, 128], P('dom')
- coarse_agg: int32 [16384], P('dom'), may hold values from 0 to 7, as said below
- coarse_inverse: float32 [1024, 1024], replicated
Outputs:
- solution: float32 [64, 524288], P(None, 'dom')
The draws below stay inside these ranges and needn't reach their ends.
Inputs may be any that keep to these rules, and one draw needn't show every extreme that they name: `block_cols`: entries below 32 name own block rows, 32 to 35 the lower neighbour's sent blocks, the rest the upper neighbour's; every sent slot is named by some block row of the receiving partition. `send_lists`: the 4 entries of each list are distinct local block rows. `fine_agg`: every aggregate of every partition holds at least one node. `coarse_agg`: every second-level aggregate of every partition holds at least one coarse node.
All inputs are finite; a program needn't handle non-finite values.
Results may differ from the reference program's by a relative error of at most 0.0001.
Values sent between devices are 32-bit elements; how exact they have to be, the bound alone decides.
A program may use at most 128 MiB of HBM per device.

```python
import math
import jax
import jax.numpy as jnp
from jax import lax

BS = 128
RHS = 64
RB = 32
NB = 3
SL = 4
AGG = 128
C2 = 8
SWEEPS = 2
CYCLES = 2
BROWS = 4096
NODES = 524288
CNODES = 16384
CN = 1024
N_DOM = 128


row_level = 4.0


noise_level = 1.5


def coupling(key, shape, columns):
    mean_part = row_level / columns
    spread = noise_level / math.sqrt(columns)
    jitter = jnp.clip(jax.random.normal(key, shape, jnp.float32), -4.0, 4.0)
    return spread * jitter - mean_part


def dominant_blocks(key, count, size, columns):
    key_off, key_diag = jax.random.split(key)
    off_part = coupling(key_off, (count, size, size), columns)
    excess = jax.random.uniform(key_diag, (count, size), jnp.float32, 0.05, 0.25)
    identity = jnp.eye(size, dtype=jnp.float32)
    diag_vals = row_level * (1.0 + excess)
    return off_part * (1.0 - identity) + diag_vals[:, :, None] * identity


def draw_diag_blocks(key, part):
    return dominant_blocks(jax.random.fold_in(key, 11), BROWS, BS, (NB + 1) * BS)


def draw_off_blocks(key, part):
    return coupling(jax.random.fold_in(key, 14), (BROWS, NB, BS, BS), (NB + 1) * BS)


def draw_coarse_diag(key, part):
    return dominant_blocks(jax.random.fold_in(key, 12), N_DOM, AGG, 3 * AGG)


def draw_coarse_side(key, part):
    return coupling(jax.random.fold_in(key, 15), (N_DOM, 2, AGG, AGG), 3 * AGG)


def draw_coarse_inverse(key, part):
    key_scale, key_noise = jax.random.split(jax.random.fold_in(key, 13))
    node_index = jnp.arange(CN, dtype=jnp.int32)
    distance = jnp.abs(node_index[:, None] - node_index[None, :])
    loop_gap = jnp.minimum(distance, CN - distance).astype(jnp.float32)
    kernel = jnp.exp(loop_gap * (math.log(0.7) / C2))
    scales = jax.random.uniform(key_scale, (N_DOM,), jnp.float32, 0.5, 1.5)
    jitter = 0.3 * jnp.clip(jax.random.normal(key_noise, (CN, CN), jnp.float32), -4.0, 4.0)
    node_scale = scales[node_index // C2]
    block_part = 0.15 / C2 * node_scale[:, None] * node_scale[None, :] * kernel
    return block_part + 0.15 * jnp.eye(CN, dtype=jnp.float32) + jitter / math.sqrt(CN)


def draw_rhs_fields(key, part):
    key_noise, key_amp, key_phase, key_wave = jax.random.split(jax.random.fold_in(key, 51), 4)
    position = jnp.arange(NODES, dtype=jnp.float32)[None, :] * (2.0 * math.pi / NODES)
    wave_count = jax.random.randint(key_wave, (RHS, 1), 1, 4, dtype=jnp.int32).astype(jnp.float32)
    offset_phase = jax.random.uniform(key_phase, (RHS, 1), jnp.float32, -math.pi, math.pi)
    amplitude = jax.random.uniform(key_amp, (RHS, 1), jnp.float32, 0.3, 0.8)
    rough_part = jnp.clip(jax.random.normal(key_noise, (RHS, NODES), jnp.float32), -4.0, 4.0)
    level = 0.6
    smooth_part = amplitude * (level + (1.0 - level) * jnp.cos(wave_count * position + offset_phase))
    return rough_part + smooth_part


def draw_block_cols(key, part):
    base = jax.random.randint(jax.random.fold_in(key, 21), (BROWS, NB), 0, RB + 2 * SL, dtype=jnp.int32)
    local = jnp.arange(BROWS, dtype=jnp.int32) % RB
    forced = local < 2 * SL
    first = jnp.where(forced, RB + local, base[:, 0])
    second = jnp.where(forced, local, base[:, 1])
    return jnp.concatenate([first[:, None], second[:, None], base[:, 2:]], axis=1).astype(jnp.int32)


def force_first(perm, value):
    swapped = jnp.where(perm == value, perm[0], perm)
    return swapped.at[0].set(value)


def draw_send_lists(key, part):
    keys = jax.random.split(jax.random.fold_in(key, 31), N_DOM * 2)
    perms = jax.vmap(lambda single: jax.random.permutation(single, RB))(keys).astype(jnp.int32)
    perms = perms.at[0].set(force_first(perms[0], 0))
    perms = perms.at[1].set(force_first(perms[1], RB - 1))
    return perms[:, :SL].reshape(N_DOM, 2, SL).astype(jnp.int32)


def local_groups(key, parts, length, groups):
    key_base, key_perm = jax.random.split(key)
    base = jax.random.randint(key_base, (parts, length), 0, groups, dtype=jnp.int32)
    keys = jax.random.split(key_perm, parts)
    perms = jax.vmap(lambda single: jax.random.permutation(single, groups))(keys).astype(jnp.int32)
    base = base.at[:, :groups].set(perms)
    return base.reshape(parts * length).astype(jnp.int32)


def draw_fine_agg(key, part):
    return local_groups(jax.random.fold_in(key, 41), N_DOM, RB * BS, AGG)


def draw_coarse_agg(key, part):
    return local_groups(jax.random.fold_in(key, 42), N_DOM, AGG, C2)


def setup_inputs(seed: int = 0) -> dict:
    arg_keys = jax.random.split(jax.random.key(seed), 11)
    rhs_fields = draw_rhs_fields(jax.random.fold_in(arg_keys[10], 71), 0)
    diag_blocks = draw_diag_blocks(jax.random.fold_in(arg_keys[10], 71), 0)
    off_blocks = draw_off_blocks(jax.random.fold_in(arg_keys[10], 71), 0)
    block_cols = draw_block_cols(jax.random.fold_in(arg_keys[10], 71), 0)
    send_lists = draw_send_lists(jax.random.fold_in(arg_keys[10], 71), 0)
    fine_agg = draw_fine_agg(jax.random.fold_in(arg_keys[10], 71), 0)
    coarse_diag = draw_coarse_diag(jax.random.fold_in(arg_keys[10], 71), 0)
    coarse_side = draw_coarse_side(jax.random.fold_in(arg_keys[10], 71), 0)
    coarse_agg = draw_coarse_agg(jax.random.fold_in(arg_keys[10], 71), 0)
    coarse_inverse = draw_coarse_inverse(jax.random.fold_in(arg_keys[10], 71), 0)
    return dict(rhs_fields=rhs_fields, diag_blocks=diag_blocks, off_blocks=off_blocks, block_cols=block_cols, send_lists=send_lists, fine_agg=fine_agg, coarse_diag=coarse_diag, coarse_side=coarse_side, coarse_agg=coarse_agg, coarse_inverse=coarse_inverse)


relax_weight = 0.6
smooth_weight = 0.5

def global_columns(block_cols, send_lists):
    devices = jnp.arange(N_DOM, dtype=jnp.int32)
    lower = (devices - 1) % N_DOM
    upper = (devices + 1) % N_DOM
    own_rows = devices[:, None] * RB + jnp.arange(RB, dtype=jnp.int32)[None, :]
    from_lower = lower[:, None] * RB + send_lists[lower, 1].astype(jnp.int32)
    from_upper = upper[:, None] * RB + send_lists[upper, 0].astype(jnp.int32)
    slot_map = jnp.concatenate([own_rows, from_lower, from_upper], axis=1)
    row_device = jnp.arange(BROWS, dtype=jnp.int32) // RB
    return slot_map[row_device[:, None], block_cols.astype(jnp.int32)]

def apply_fine(field, diag_blocks, off_blocks, columns):
    blocks_view = field.reshape(RHS, BROWS, BS)
    result = jnp.einsum('iab,rib->ria', diag_blocks, blocks_view, precision=lax.Precision.HIGHEST)
    picked = blocks_view[:, columns, :]
    result = result + jnp.einsum('ikab,rikb->ria', off_blocks, picked, precision=lax.Precision.HIGHEST)
    return result.reshape(RHS, NODES)

def apply_coarse(field, coarse_diag, coarse_side):
    view = field.reshape(RHS, N_DOM, AGG)
    below = jnp.roll(view, 1, axis=1)
    above = jnp.roll(view, -1, axis=1)
    hp = lax.Precision.HIGHEST
    result = jnp.einsum('pab,rpb->rpa', coarse_diag, view, precision=hp)
    result = result + jnp.einsum('pab,rpb->rpa', coarse_side[:, 0], below, precision=hp)
    result = result + jnp.einsum('pab,rpb->rpa', coarse_side[:, 1], above, precision=hp)
    return result.reshape(RHS, CNODES)

def reference(rhs_fields, diag_blocks, off_blocks, block_cols, send_lists, fine_agg, coarse_diag, coarse_side, coarse_agg, coarse_inverse):
    columns = global_columns(block_cols, send_lists)
    dinv = 1.0 / jnp.diagonal(diag_blocks, axis1=1, axis2=2).reshape(NODES)
    d1inv = 1.0 / jnp.diagonal(coarse_diag, axis1=1, axis2=2).reshape(CNODES)
    group_one = jnp.arange(NODES, dtype=jnp.int32) // (RB * BS) * AGG + fine_agg.astype(jnp.int32)
    count_one = jax.ops.segment_sum(jnp.ones((NODES,), jnp.float32), group_one, CNODES)
    scale_one = 1.0 / jnp.sqrt(count_one)
    group_two = jnp.arange(CNODES, dtype=jnp.int32) // AGG * C2 + coarse_agg.astype(jnp.int32)
    count_two = jax.ops.segment_sum(jnp.ones((CNODES,), jnp.float32), group_two, CN)
    scale_two = 1.0 / jnp.sqrt(count_two)

    def fine_op(field):
        return apply_fine(field, diag_blocks, off_blocks, columns)

    def coarse_op(field):
        return apply_coarse(field, coarse_diag, coarse_side)

    def coarse_cycle(right_one):
        iterate = jnp.zeros((RHS, CNODES), jnp.float32)
        for sweep_index in range(SWEEPS):
            iterate = iterate + relax_weight * d1inv * (right_one - coarse_op(iterate))
        resid_one = right_one - coarse_op(iterate)
        resid_two = jax.ops.segment_sum(resid_one.T, group_two, CN).T * scale_two
        correction = jnp.dot(resid_two, coarse_inverse.T, precision=lax.Precision.HIGHEST)
        iterate = iterate + (correction * scale_two)[:, group_two]
        for sweep_index in range(SWEEPS):
            iterate = iterate + relax_weight * d1inv * (right_one - coarse_op(iterate))
        return iterate
    solution = jnp.zeros((RHS, NODES), jnp.float32)
    for cycle_index in range(CYCLES):
        for sweep_index in range(SWEEPS):
            solution = solution + relax_weight * dinv * (rhs_fields - fine_op(solution))
        resid = rhs_fields - fine_op(solution)
        smoothed = resid - smooth_weight * fine_op(dinv * resid)
        right_one = jax.ops.segment_sum(smoothed.T, group_one, CNODES).T * scale_one
        coarse_sol = coarse_cycle(right_one)
        lifted = (coarse_sol * scale_one)[:, group_one]
        solution = solution + lifted - smooth_weight * dinv * fine_op(lifted)
        for sweep_index in range(SWEEPS):
            solution = solution + relax_weight * dinv * (rhs_fields - fine_op(solution))
    return solution
```

```python
import jax
import jax.numpy as jnp
from jax import lax
from jax.experimental import pallas as pl
from jax.experimental.pallas import tpu as pltpu
from jax.sharding import PartitionSpec as P

MESH = pl.DeviceIdType.MESH
RELAX = 0.6
SMOOTH = 0.5
F32 = jnp.float32
BF16 = jnp.bfloat16
CHUNK = 4


def split(x):
    hi = x.astype(BF16)
    lo = (x - hi.astype(F32)).astype(BF16)
    return jnp.concatenate([hi, lo], axis=0)


def split_columns(x):
    hi = x.astype(BF16)
    lo = (x - hi.astype(F32)).astype(BF16)
    return jnp.concatenate([hi, lo], axis=1)


def fold(res, rows, width):
    return res[:rows, :width] + res[:rows, width:] + res[rows:, :width]


def kernel(
    cols_in, lists_in,
    rhs_hbm, diag_hbm, off_hbm, agg_ref, cdiag_ref, cside_ref, cagg_ref, inv_hbm,
    out_ref,
    perm, pos, cols, sent_pos,
    rhs_v, diag_v, off_v, inv_v, weights, xs, x_ref, r_ref, u_ref, f_ref, dnat, dinv, table, tbuf,
    first8, send, recv, cw, cx, csend, crecv, inv_s, gtile, gather, gfull,
    load_sem, off_sem, send_sem, recv_sem, csend_sem, crecv_sem, gsend_sem, grecv_sem,
):
    nright, nrows, width = f_ref.shape[1], f_ref.shape[0], f_ref.shape[2]
    me = lax.axis_index("dom")
    count = 128
    upper = lax.rem(me + 1, count)
    lower = lax.rem(me + count - 1, count)
    core = lax.rem(me, 2)
    y = lax.rem(me // 2, 4)
    z = lax.rem(me // 8, 4)
    xc = me // 32
    partner = me + 1 - 2 * core

    def member(ax, step):
        if ax == 0:
            return me + 2 * (lax.rem(y + step, 4) - y)
        if ax == 1:
            return me + 8 * (lax.rem(z + step, 4) - z)
        return me + 32 * (lax.rem(xc + step, 4) - xc)

    load_rhs = pltpu.make_async_copy(rhs_hbm, rhs_v, load_sem.at[0])
    load_diag = pltpu.make_async_copy(diag_hbm, diag_v, load_sem.at[1])
    load_inv = pltpu.make_async_copy(
        inv_hbm.at[pl.ds(pl.multiple_of(me * 8, 8), 8)], inv_v, load_sem.at[2]
    )
    load_diag.start()
    load_rhs.start()

    def load_off(c):
        rows = pl.ds(c * CHUNK, CHUNK)
        return pltpu.make_async_copy(off_hbm.at[rows], off_v.at[rows], off_sem.at[c])

    for c in range(nrows // CHUNK):
        load_off(c).start()
    load_inv.start()

    barrier = pltpu.get_barrier_semaphore()
    peers = [upper, lower] + [member(ax, s) for ax in range(3) for s in (1, 2, 3)]
    for peer in peers:
        pl.semaphore_signal(barrier, inc=1, device_id=(peer,), device_id_type=MESH)

    wanted = [lists_in[m] for m in range(8)]

    def count_sent(i, total):
        flag = wanted[0] == i
        for m in range(1, 8):
            flag = jnp.logical_or(flag, wanted[m] == i)
        value = flag.astype(jnp.int32)
        pos[i] = value
        return total + value

    nsent = lax.fori_loop(0, nrows, count_sent, jnp.int32(0))

    def place(i, carry):
        a, b = carry
        value = pos[i]
        pos[i] = jnp.where(value == 1, a, b)
        return a + value, b + 1 - value

    lax.fori_loop(0, nrows, place, (jnp.int32(0), nsent))

    def invert(j, _):
        total = jnp.int32(0)
        for i in range(nrows):
            total = total + jnp.where(pos[i] == j, i, 0)
        perm[j] = total
        for k in range(3):
            c = cols_in[total * 3 + k]
            own = pos[jnp.minimum(c, nrows - 1)]
            cols[j * 3 + k] = jnp.where(c < nrows, own, c)
        return 0

    lax.fori_loop(0, nrows, invert, 0)
    for m in range(8):
        sent_pos[m] = pos[wanted[m]]

    def halo_copies(n):
        slot = lax.rem(n, 3)
        up = pltpu.make_async_remote_copy(
            src_ref=send.at[slot, 1], dst_ref=recv.at[slot, 0],
            send_sem=send_sem.at[slot, 1], recv_sem=recv_sem.at[slot, 0],
            device_id=(upper,), device_id_type=MESH,
        )
        down = pltpu.make_async_remote_copy(
            src_ref=send.at[slot, 0], dst_ref=recv.at[slot, 1],
            send_sem=send_sem.at[slot, 0], recv_sem=recv_sem.at[slot, 1],
            device_id=(lower,), device_id_type=MESH,
        )
        return up, down

    def halo_send(n):
        slot = lax.rem(n, 3)
        for m in range(8):
            send[slot, m // 4, m % 4] = first8[sent_pos[m]]
        up, down = halo_copies(n)
        up.start()
        down.start()

    def halo_sent(n):
        for copy in halo_copies(n):
            copy.wait_send()

    def halo_take(n):
        slot, par = lax.rem(n, 3), lax.rem(n, 2)
        for copy in halo_copies(n):
            copy.wait_recv()
        for m in range(8):
            xs[par, nrows + m] = split(recv[slot, m // 4, m % 4])

    def product(par, j):
        parts = [xs[par, j]] + [xs[par, cols[j * 3 + k]] for k in range(3)]
        res = jnp.dot(
            jnp.concatenate(parts, axis=1), weights[perm[j]], preferred_element_type=F32
        )
        return fold(res, nright, width)

    def rows_first(body):
        for j in range(8):
            body(j, j)

    def rows_rest(body):
        def step(g, _):
            for u in range(8):
                body(8 + g * 8 + u, None)
            return 0

        lax.fori_loop(0, (nrows - 8) // 8, step, 0)

    def publish(par, j, fixed, v):
        xs[1 - par, j] = split(v)
        if fixed is not None:
            first8[fixed] = v

    rows_iota = lax.broadcasted_iota(jnp.int32, (width, width), 0)
    eye = rows_iota == lax.broadcasted_iota(jnp.int32, (width, width), 1)
    load_diag.wait()

    def take_diag(i, _):
        d = jnp.sum(jnp.where(eye, diag_v[i], 0.0), axis=0, keepdims=True)
        dnat[i] = 1.0 / d
        return 0

    lax.fori_loop(0, nrows, take_diag, 0)
    load_rhs.wait()
    for i in range(nrows):
        u_ref[i] = rhs_v[:, i * width:(i + 1) * width]

    def start_row(j, fixed):
        d = dnat[perm[j]]
        dinv[j] = d
        f = u_ref[perm[j]]
        f_ref[j] = f
        v = RELAX * d * f
        x_ref[j] = v
        publish(jnp.int32(1), j, fixed, v)

    rows_first(start_row)
    pl.semaphore_wait(barrier, len(peers))
    halo_send(jnp.int32(0))
    rows_rest(start_row)

    def convert(c, _):
        load_off(c).wait()
        for q in range(CHUNK):
            i = c * CHUNK + q
            weights[i, 0:width] = split_columns(diag_v[i].T)
            for k in range(3):
                weights[i, (k + 1) * width:(k + 2) * width] = split_columns(off_v[i, k].T)
        return 0

    lax.fori_loop(0, nrows // CHUNK, convert, 0)

    def make_table(j, sums):
        hot = (agg_ref[perm[j]] == rows_iota).astype(F32)
        table[j] = hot.astype(BF16)
        return sums + hot

    sums = lax.fori_loop(0, nrows, make_table, jnp.zeros((width, width), F32))
    count_one = jnp.sum(sums, axis=1, keepdims=True)
    scale_one = (1.0 / jnp.sqrt(jnp.broadcast_to(count_one, (width, width)))).T[0:1]
    hot_two = (cagg_ref[...] == lax.broadcasted_iota(jnp.int32, (8, width), 0)).astype(F32)
    table_two = hot_two * (1.0 / jnp.sqrt(jnp.sum(hot_two, axis=1, keepdims=True)))
    table_two_pad = jnp.concatenate([table_two, jnp.zeros((width - 8, width), F32)], axis=0)
    cd = cdiag_ref[0]
    d1inv = 1.0 / jnp.sum(jnp.where(eye, cd, 0.0), axis=0, keepdims=True)
    cw[0:width] = split_columns(cd.T)
    cw[width:2 * width] = split_columns(cside_ref[0, 0].T)
    cw[2 * width:3 * width] = split_columns(cside_ref[0, 1].T)
    load_inv.wait()
    inv_s[...] = split(inv_v[...])

    def coarse_copies(m):
        slot = lax.rem(m, 3)
        up = pltpu.make_async_remote_copy(
            src_ref=csend.at[slot], dst_ref=crecv.at[slot, 0],
            send_sem=csend_sem.at[slot, 1], recv_sem=crecv_sem.at[slot, 0],
            device_id=(upper,), device_id_type=MESH,
        )
        down = pltpu.make_async_remote_copy(
            src_ref=csend.at[slot], dst_ref=crecv.at[slot, 1],
            send_sem=csend_sem.at[slot, 0], recv_sem=crecv_sem.at[slot, 1],
            device_id=(lower,), device_id_type=MESH,
        )
        return up, down

    def coarse_op(value, m):
        slot = lax.rem(m, 3)
        csend[slot] = value
        copies = coarse_copies(m)
        for copy in copies:
            copy.start()
        for copy in copies:
            copy.wait()
        lhs = jnp.concatenate(
            [split(value), split(crecv[slot, 0]), split(crecv[slot, 1])], axis=1
        )
        return fold(jnp.dot(lhs, cw[...], preferred_element_type=F32), nright, width)

    chip = me // 2

    def gather_copies(cyc, ax):
        size = (1, 4, 16)[ax]
        first = (chip // size) * size
        out = []
        for s in (1, 2, 3):
            where = gather.at[cyc, pl.ds(first, size)]
            out.append(pltpu.make_async_remote_copy(
                src_ref=where, dst_ref=where,
                send_sem=gsend_sem.at[cyc, ax * 3 + s], recv_sem=grecv_sem.at[cyc, ax * 3 + s],
                device_id=(member(ax, s),), device_id_type=MESH,
            ))
        return out

    def gather_waits(cyc, ax):
        size = (1, 4, 16)[ax]
        for s in (1, 2, 3):
            source = member(ax, 4 - s) // 2
            where = gather.at[cyc, pl.ds((source // size) * size, size)]
            pltpu.make_async_remote_copy(
                src_ref=where, dst_ref=where,
                send_sem=gsend_sem.at[cyc, ax * 3 + s], recv_sem=grecv_sem.at[cyc, ax * 3 + s],
                device_id=(member(ax, s),), device_id_type=MESH,
            ).wait_recv()

    def gather_all(cyc, tile):
        gtile[cyc, 0] = tile
        pair = pltpu.make_async_remote_copy(
            src_ref=gtile.at[cyc, 0], dst_ref=gtile.at[cyc, 1],
            send_sem=gsend_sem.at[cyc, 0], recv_sem=grecv_sem.at[cyc, 0],
            device_id=(partner,), device_id_type=MESH,
        )
        pair.start()
        pair.wait()
        other = gtile[cyc, 1]
        even = jnp.where(core == 0, tile, other)
        odd = jnp.where(core == 0, other, tile)
        low_lanes = lax.broadcasted_iota(jnp.int32, (8, width), 1) < nright
        gather[cyc, pl.ds(chip, 1)] = jnp.where(low_lanes, even, pltpu.roll(odd, nright, 1))[None]
        for ax in range(3):
            copies = gather_copies(cyc, ax)
            for copy in copies:
                copy.start()
            gather_waits(cyc, ax)
            for copy in copies:
                copy.wait_send()
        for c in range(64):
            pair_tile = gather[cyc, c]
            gfull[16 * c:16 * c + 8] = split_columns(pair_tile)
            gfull[16 * c + 8:16 * c + 16] = split_columns(pltpu.roll(pair_tile, nright, 1))

    def sweep(n, last):
        par = lax.rem(n, 2)
        halo_take(n)

        def body(j, fixed):
            d = RELAX * dinv[j]
            new = x_ref[j] + d * (f_ref[j] - product(par, j))
            x_ref[j] = new
            publish(par, j, fixed, new)

        rows_first(body)
        if last is None:
            halo_send(n + 1)
        else:
            @pl.when(n < last)
            def _():
                halo_send(n + 1)
        rows_rest(body)
        if last is None:
            halo_sent(n + 1)
        else:
            @pl.when(n < last)
            def _():
                halo_sent(n + 1)

    halo_sent(jnp.int32(0))
    sweep(jnp.int32(0), None)

    def cycle(cyc, _):
        n = 1 + 7 * cyc
        par = lax.rem(n, 2)
        halo_take(n)

        def resid_row(j, fixed):
            r = f_ref[j] - product(par, j)
            r_ref[j] = r
            publish(par, j, fixed, dinv[j] * r)

        rows_first(resid_row)
        halo_send(n + 1)
        rows_rest(resid_row)
        halo_sent(n + 1)

        n1 = n + 1
        par1 = lax.rem(n1, 2)
        halo_take(n1)

        def smooth_row(j, fixed):
            tbuf[j] = split(r_ref[j] - SMOOTH * product(par1, j))

        rows_first(smooth_row)
        rows_rest(smooth_row)

        def restrict(g, acc):
            for u in range(8):
                j = g * 8 + u
                acc = acc + lax.dot_general(
                    tbuf[j], table[j], (((1,), (1,)), ((), ())), preferred_element_type=F32
                )
            return acc

        acc = lax.fori_loop(0, nrows // 8, restrict, jnp.zeros((2 * nright, width), F32))
        right_one = (acc[:nright] + acc[nright:]) * scale_one

        m = 4 * cyc
        it = RELAX * d1inv * right_one
        it = it + RELAX * d1inv * (right_one - coarse_op(it, m))
        resid_one = right_one - coarse_op(it, m + 1)
        padded = jnp.concatenate([resid_one, jnp.zeros((width - nright, width), F32)], axis=0)
        tile = lax.dot_general(
            table_two, padded, (((1,), (1,)), ((), ())),
            precision=lax.Precision.HIGHEST, preferred_element_type=F32,
        )
        gather_all(cyc, tile)
        e2 = fold(jnp.dot(inv_s[...], gfull[...], preferred_element_type=F32), 8, width)
        e2t = jnp.concatenate([e2, jnp.zeros((width - 8, width), F32)], axis=0).T[:nright]
        it = it + jnp.dot(
            e2t, table_two_pad, precision=lax.Precision.HIGHEST, preferred_element_type=F32
        )
        it = it + RELAX * d1inv * (right_one - coarse_op(it, m + 2))
        it = it + RELAX * d1inv * (right_one - coarse_op(it, m + 3))
        cx[...] = split(it * scale_one)

        n2 = n + 2
        par2 = lax.rem(n2, 2)

        def lift_row(j, fixed):
            res = jnp.dot(cx[...], table[j], preferred_element_type=F32)
            u = res[:nright] + res[nright:]
            u_ref[j] = u
            publish(1 - par2, j, fixed, u)

        rows_first(lift_row)
        halo_send(n2)
        rows_rest(lift_row)
        halo_sent(n2)
        halo_take(n2)

        def correct_row(j, fixed):
            d = SMOOTH * dinv[j]
            new = x_ref[j] + u_ref[j] - d * product(par2, j)
            x_ref[j] = new
            publish(par2, j, fixed, new)

        rows_first(correct_row)
        halo_send(n2 + 1)
        rows_rest(correct_row)
        halo_sent(n2 + 1)

        def sweeps(s, _):
            sweep(n2 + 1 + s, 12)
            return 0

        lax.fori_loop(0, 4 - 2 * cyc, sweeps, 0)
        return 0

    lax.fori_loop(0, 2, cycle, 0)
    for i in range(nrows):
        out_ref[:, i * width:(i + 1) * width] = x_ref[pos[i]]


def local(
    rhs_fields, diag_blocks, off_blocks, block_cols, send_lists, fine_agg,
    coarse_diag, coarse_side, coarse_agg, coarse_inverse,
):
    nrows, width = diag_blocks.shape[0], diag_blocks.shape[1]
    nright = rhs_fields.shape[0]
    naggs = coarse_diag.shape[1]
    S = pl.BlockSpec(memory_space=pltpu.SMEM)
    V = pl.BlockSpec(memory_space=pltpu.VMEM)
    A = pl.BlockSpec(memory_space=pl.ANY)
    DMA = pltpu.SemaphoreType.DMA
    return pl.pallas_call(
        kernel,
        name="multigrid",
        out_shape=jax.ShapeDtypeStruct(rhs_fields.shape, F32),
        in_specs=[S, S, A, A, A, V, V, V, V, A],
        out_specs=V,
        scratch_shapes=[
            pltpu.SMEM((nrows,), jnp.int32),
            pltpu.SMEM((nrows,), jnp.int32),
            pltpu.SMEM((3 * nrows,), jnp.int32),
            pltpu.SMEM((8,), jnp.int32),
            pltpu.VMEM(rhs_fields.shape, F32),
            pltpu.VMEM(diag_blocks.shape, F32),
            pltpu.VMEM(off_blocks.shape, F32),
            pltpu.VMEM((8, coarse_inverse.shape[1]), F32),
            pltpu.VMEM((nrows, 4 * width, 2 * width), BF16),
            pltpu.VMEM((2, nrows + 8, 2 * nright, width), BF16),
            pltpu.VMEM((nrows, nright, width), F32),
            pltpu.VMEM((nrows, nright, width), F32),
            pltpu.VMEM((nrows, nright, width), F32),
            pltpu.VMEM((nrows, nright, width), F32),
            pltpu.VMEM((nrows, 1, width), F32),
            pltpu.VMEM((nrows, 1, width), F32),
            pltpu.VMEM((nrows, naggs, width), BF16),
            pltpu.VMEM((nrows, 2 * nright, width), BF16),
            pltpu.VMEM((8, nright, width), F32),
            pltpu.VMEM((3, 2, 4, nright, width), F32),
            pltpu.VMEM((3, 2, 4, nright, width), F32),
            pltpu.VMEM((3 * width, 2 * width), BF16),
            pltpu.VMEM((2 * nright, width), BF16),
            pltpu.VMEM((3, nright, width), F32),
            pltpu.VMEM((3, 2, nright, width), F32),
            pltpu.VMEM((16, coarse_inverse.shape[1]), BF16),
            pltpu.VMEM((2, 2, 8, width), F32),
            pltpu.VMEM((2, 64, 8, width), F32),
            pltpu.VMEM((1024, 2 * width), BF16),
            DMA((3,)),
            DMA((nrows // CHUNK,)),
            DMA((3, 2)),
            DMA((3, 2)),
            DMA((3, 2)),
            DMA((3, 2)),
            DMA((2, 10)),
            DMA((2, 10)),
        ],
        compiler_params=pltpu.CompilerParams(
            collective_id=0, has_side_effects=True, vmem_limit_bytes=60 * 1024 * 1024
        ),
    )(
        block_cols.reshape(-1), send_lists.reshape(-1),
        rhs_fields, diag_blocks, off_blocks, fine_agg.reshape(nrows, 1, width),
        coarse_diag, coarse_side, coarse_agg.reshape(1, naggs), coarse_inverse,
    )


def solution(mesh):
    return jax.shard_map(
        local,
        mesh=mesh,
        in_specs=(
            P(None, "dom"),
            P("dom", None, None),
            P("dom", None, None, None),
            P("dom", None),
            P("dom", None, None),
            P("dom"),
            P("dom", None, None),
            P("dom", None, None, None),
            P("dom"),
            P(),
        ),
        out_specs=P(None, "dom"),
        check_vma=False,
    )
```

```python
import jax
import jax.numpy as jnp
from jax import lax
from jax.experimental import pallas as pl
from jax.experimental.pallas import tpu as pltpu
from jax.sharding import PartitionSpec as P

MESH = pl.DeviceIdType.MESH
RELAX = 0.6
SMOOTH = 0.5
F32 = jnp.float32
BF16 = jnp.bfloat16
CHUNK = 4
OFFSETS = (1, -1, 2, -2, 3, -3, 4, -4)


def split(x):
    hi = x.astype(BF16)
    lo = (x - hi.astype(F32)).astype(BF16)
    return jnp.concatenate([hi, lo], axis=0)


def split_columns(x):
    hi = x.astype(BF16)
    lo = (x - hi.astype(F32)).astype(BF16)
    return jnp.concatenate([hi, lo], axis=1)


def fold(res, rows, width):
    return res[:rows, :width] + res[:rows, width:] + res[rows:, :width]


def kernel(
    cols_in, lists_in,
    rhs_hbm, diag_hbm, off_hbm, agg_ref, cdiag_ref, cside_ref, cagg_ref, inv_hbm,
    out_ref,
    perm, pos, cols, sent_pos,
    rhs_v, diag_v, off_v, inv_v, weights, xs, x_ref, r_ref, u_ref, f_ref, dnat, dinv, table, tbuf,
    first8, send, recv, cw, cx, small, big_diag, big_side, fbuf, tw, near_table, inv_s,
    gtile, gather, gfull,
    load_sem, off_sem, send_sem, recv_sem, small_send, small_recv, big_send, big_recv,
    fsend_sem, frecv_sem, gsend_sem, grecv_sem,
):
    nright, nrows, width = f_ref.shape[1], f_ref.shape[0], f_ref.shape[2]
    me = lax.axis_index("dom")
    count = 128
    upper = lax.rem(me + 1, count)
    lower = lax.rem(me + count - 1, count)
    core = lax.rem(me, 2)
    y = lax.rem(me // 2, 4)
    z = lax.rem(me // 8, 4)
    xc = me // 32
    partner = me + 1 - 2 * core

    def member(ax, step):
        if ax == 0:
            return me + 2 * (lax.rem(y + step, 4) - y)
        if ax == 1:
            return me + 8 * (lax.rem(z + step, 4) - z)
        return me + 32 * (lax.rem(xc + step, 4) - xc)

    load_rhs = pltpu.make_async_copy(rhs_hbm, rhs_v, load_sem.at[0])
    load_diag = pltpu.make_async_copy(diag_hbm, diag_v, load_sem.at[1])
    def at_offset(o):
        return lax.rem(me + o + count, count)

    load_inv = [
        pltpu.make_async_copy(
            inv_hbm.at[pl.ds(pl.multiple_of(at_offset(o) * 8, 8), 8)],
            inv_v.at[o + 3], load_sem.at[5 + o],
        )
        for o in range(-3, 4)
    ]
    load_diag.start()
    load_rhs.start()

    def load_off(c):
        rows = pl.ds(c * CHUNK, CHUNK)
        return pltpu.make_async_copy(off_hbm.at[rows], off_v.at[rows], off_sem.at[c])

    for c in range(nrows // CHUNK):
        load_off(c).start()
    for load in load_inv:
        load.start()

    barrier = pltpu.get_barrier_semaphore()
    peers = [at_offset(o) for o in OFFSETS] + [member(ax, s) for ax in range(3) for s in (1, 2, 3)]
    for peer in peers:
        pl.semaphore_signal(barrier, inc=1, device_id=(peer,), device_id_type=MESH)

    wanted = [lists_in[m] for m in range(8)]

    def count_sent(i, total):
        flag = wanted[0] == i
        for m in range(1, 8):
            flag = jnp.logical_or(flag, wanted[m] == i)
        value = flag.astype(jnp.int32)
        pos[i] = value
        return total + value

    nsent = lax.fori_loop(0, nrows, count_sent, jnp.int32(0))

    def place(i, carry):
        a, b = carry
        value = pos[i]
        pos[i] = jnp.where(value == 1, a, b)
        return a + value, b + 1 - value

    lax.fori_loop(0, nrows, place, (jnp.int32(0), nsent))

    def invert(j, _):
        total = jnp.int32(0)
        for i in range(nrows):
            total = total + jnp.where(pos[i] == j, i, 0)
        perm[j] = total
        for k in range(3):
            c = cols_in[total * 3 + k]
            own = pos[jnp.minimum(c, nrows - 1)]
            cols[j * 3 + k] = jnp.where(c < nrows, own, c)
        return 0

    lax.fori_loop(0, nrows, invert, 0)
    for m in range(8):
        sent_pos[m] = pos[wanted[m]]

    def halo_copies(n):
        slot = lax.rem(n, 3)
        up = pltpu.make_async_remote_copy(
            src_ref=send.at[slot, 1], dst_ref=recv.at[slot, 0],
            send_sem=send_sem.at[slot, 1], recv_sem=recv_sem.at[slot, 0],
            device_id=(upper,), device_id_type=MESH,
        )
        down = pltpu.make_async_remote_copy(
            src_ref=send.at[slot, 0], dst_ref=recv.at[slot, 1],
            send_sem=send_sem.at[slot, 0], recv_sem=recv_sem.at[slot, 1],
            device_id=(lower,), device_id_type=MESH,
        )
        return up, down

    def halo_send(n):
        slot = lax.rem(n, 3)
        for m in range(8):
            send[slot, m // 4, m % 4] = first8[sent_pos[m]]
        up, down = halo_copies(n)
        up.start()
        down.start()

    def halo_sent(n):
        for copy in halo_copies(n):
            copy.wait_send()

    def halo_take(n):
        slot, par = lax.rem(n, 3), lax.rem(n, 2)
        for copy in halo_copies(n):
            copy.wait_recv()
        for m in range(8):
            xs[par, nrows + m] = split(recv[slot, m // 4, m % 4])

    def product(par, j):
        parts = [xs[par, j]] + [xs[par, cols[j * 3 + k]] for k in range(3)]
        res = jnp.dot(
            jnp.concatenate(parts, axis=1), weights[perm[j]], preferred_element_type=F32
        )
        return fold(res, nright, width)

    def rows_first(body):
        for j in range(8):
            body(j, j)

    def rows_rest(body):
        def step(g, _):
            for u in range(8):
                body(8 + g * 8 + u, None)
            return 0

        lax.fori_loop(0, (nrows - 8) // 8, step, 0)

    def publish(par, j, fixed, v):
        xs[1 - par, j] = split(v)
        if fixed is not None:
            first8[fixed] = v

    rows_iota = lax.broadcasted_iota(jnp.int32, (width, width), 0)
    eye = rows_iota == lax.broadcasted_iota(jnp.int32, (width, width), 1)
    load_diag.wait()

    def take_diag(i, _):
        d = jnp.sum(jnp.where(eye, diag_v[i], 0.0), axis=0, keepdims=True)
        dnat[i] = 1.0 / d
        return 0

    lax.fori_loop(0, nrows, take_diag, 0)
    load_rhs.wait()
    for i in range(nrows):
        u_ref[i] = rhs_v[:, i * width:(i + 1) * width]

    def start_row(j, fixed):
        d = dnat[perm[j]]
        dinv[j] = d
        f = u_ref[perm[j]]
        f_ref[j] = f
        v = RELAX * d * f
        x_ref[j] = v
        publish(jnp.int32(1), j, fixed, v)

    rows_first(start_row)
    pl.semaphore_wait(barrier, len(peers))
    halo_send(jnp.int32(0))
    rows_rest(start_row)

    def big_copies(o):
        return [
            pltpu.make_async_remote_copy(
                src_ref=src, dst_ref=dst.at[3 - o],
                send_sem=big_send.at[i, 3 - o], recv_sem=big_recv.at[i, 3 - o],
                device_id=(at_offset(o),), device_id_type=MESH,
            )
            for i, (src, dst) in enumerate(
                [(cdiag_ref.at[0], big_diag), (cside_ref.at[0], big_side)]
            )
        ]

    for o in OFFSETS[:6]:
        for copy in big_copies(o):
            copy.start()

    def convert(c, _):
        load_off(c).wait()
        for q in range(CHUNK):
            i = c * CHUNK + q
            weights[i, 0:width] = split_columns(diag_v[i].T)
            for k in range(3):
                weights[i, (k + 1) * width:(k + 2) * width] = split_columns(off_v[i, k].T)
        return 0

    lax.fori_loop(0, nrows // CHUNK, convert, 0)

    def make_table(j, sums):
        hot = (agg_ref[perm[j]] == rows_iota).astype(F32)
        table[j] = hot.astype(BF16)
        return sums + hot

    sums = lax.fori_loop(0, nrows, make_table, jnp.zeros((width, width), F32))
    count_one = jnp.sum(sums, axis=1, keepdims=True)
    scale_one = (1.0 / jnp.sqrt(jnp.broadcast_to(count_one, (width, width)))).T[0:1]
    hot_two = (cagg_ref[...] == lax.broadcasted_iota(jnp.int32, (8, width), 0)).astype(F32)
    table_two = hot_two * (1.0 / jnp.sqrt(jnp.sum(hot_two, axis=1, keepdims=True)))
    cd = cdiag_ref[0]
    d1inv = 1.0 / jnp.sum(jnp.where(eye, cd, 0.0), axis=0, keepdims=True)
    lists = [agg_ref[wanted[m]].astype(F32) for m in range(8)]
    small[4] = jnp.concatenate(
        [d1inv, scale_one, cagg_ref[...].astype(F32), jnp.zeros((1, width), F32)]
        + lists + [jnp.zeros((4, width), F32)],
        axis=0,
    )

    def small_copy(o):
        return pltpu.make_async_remote_copy(
            src_ref=small.at[4], dst_ref=small.at[4 - o],
            send_sem=small_send.at[4 - o], recv_sem=small_recv.at[4 - o],
            device_id=(at_offset(o),), device_id_type=MESH,
        )

    for o in OFFSETS:
        small_copy(o).start()
    big_diag[3] = cd
    big_side[3] = cside_ref[0]
    for load in load_inv:
        load.wait()
    inv_s[...] = split(jnp.concatenate([inv_v[k] for k in range(7)], axis=0))
    float_rows = rows_iota.astype(F32)

    def take_near():
        for o in OFFSETS[:6]:
            for copy in big_copies(o):
                copy.wait()
        for o in OFFSETS:
            small_copy(o).wait()

        def weigh(k, _):
            cw[k, 0:width] = split_columns(big_diag[k].T)
            cw[k, width:2 * width] = split_columns(big_side[k, 0].T)
            cw[k, 2 * width:3 * width] = split_columns(big_side[k, 1].T)
            shift = (8 * k).astype(F32)
            hot = ((small[k + 1, 2:3] + shift) == float_rows).astype(F32)
            members = jnp.maximum(jnp.sum(hot, axis=1, keepdims=True), 1.0)
            tw[k] = split_columns(hot * (1.0 / jnp.sqrt(members)))
            return 0

        lax.fori_loop(0, 7, weigh, 0)
        for m in range(4):
            near_table[m] = (small[3, 8 + m:9 + m] == float_rows).astype(BF16)
            near_table[4 + m] = (small[5, 4 + m:5 + m] == float_rows).astype(BF16)

    def coarse_copy(cyc, o):
        return pltpu.make_async_remote_copy(
            src_ref=fbuf.at[cyc, 4], dst_ref=fbuf.at[cyc, 4 - o],
            send_sem=fsend_sem.at[cyc, 4 - o], recv_sem=frecv_sem.at[cyc, 4 - o],
            device_id=(at_offset(o),), device_id_type=MESH,
        )

    def coarse_op(o, parts):
        lhs = jnp.concatenate([parts[o], parts[o - 1], parts[o + 1]], axis=1)
        return fold(jnp.dot(lhs, cw[o + 3], preferred_element_type=F32), nright, width)

    chip = me // 2

    def gather_copies(cyc, ax):
        size = (1, 4, 16)[ax]
        first = (chip // size) * size
        out = []
        for s in (1, 2, 3):
            where = gather.at[cyc, pl.ds(first, size)]
            out.append(pltpu.make_async_remote_copy(
                src_ref=where, dst_ref=where,
                send_sem=gsend_sem.at[cyc, ax * 3 + s], recv_sem=grecv_sem.at[cyc, ax * 3 + s],
                device_id=(member(ax, s),), device_id_type=MESH,
            ))
        return out

    def gather_waits(cyc, ax):
        size = (1, 4, 16)[ax]
        for s in (1, 2, 3):
            source = member(ax, 4 - s) // 2
            where = gather.at[cyc, pl.ds((source // size) * size, size)]
            pltpu.make_async_remote_copy(
                src_ref=where, dst_ref=where,
                send_sem=gsend_sem.at[cyc, ax * 3 + s], recv_sem=grecv_sem.at[cyc, ax * 3 + s],
                device_id=(member(ax, s),), device_id_type=MESH,
            ).wait_recv()

    def gather_all(cyc, tile, between):
        gtile[cyc, 0] = tile
        pair = pltpu.make_async_remote_copy(
            src_ref=gtile.at[cyc, 0], dst_ref=gtile.at[cyc, 1],
            send_sem=gsend_sem.at[cyc, 0], recv_sem=grecv_sem.at[cyc, 0],
            device_id=(partner,), device_id_type=MESH,
        )
        pair.start()
        pair.wait()
        other = gtile[cyc, 1]
        even = jnp.where(core == 0, tile, other)
        odd = jnp.where(core == 0, other, tile)
        low_lanes = lax.broadcasted_iota(jnp.int32, (8, width), 1) < nright
        gather[cyc, pl.ds(chip, 1)] = jnp.where(low_lanes, even, pltpu.roll(odd, nright, 1))[None]
        for ax in range(3):
            copies = gather_copies(cyc, ax)
            for copy in copies:
                copy.start()
            gather_waits(cyc, ax)
            for copy in copies:
                copy.wait_send()
            if ax == 0:
                between()
        for c in range(64):
            pair_tile = gather[cyc, c]
            gfull[16 * c:16 * c + 8] = split_columns(pair_tile)
            gfull[16 * c + 8:16 * c + 16] = split_columns(pltpu.roll(pair_tile, nright, 1))

    def sweep(n, last):
        par = lax.rem(n, 2)
        halo_take(n)

        def body(j, fixed):
            d = RELAX * dinv[j]
            new = x_ref[j] + d * (f_ref[j] - product(par, j))
            x_ref[j] = new
            publish(par, j, fixed, new)

        rows_first(body)
        if last is None:
            halo_send(n + 1)
        else:
            @pl.when(n < last)
            def _():
                halo_send(n + 1)
        rows_rest(body)
        if last is None:
            halo_sent(n + 1)
        else:
            @pl.when(n < last)
            def _():
                halo_sent(n + 1)

    halo_sent(jnp.int32(0))
    sweep(jnp.int32(0), None)
    take_near()

    def cycle(cyc, _):
        n = 1 + 7 * cyc
        par = lax.rem(n, 2)
        halo_take(n)

        def resid_row(j, fixed):
            r = f_ref[j] - product(par, j)
            r_ref[j] = r
            publish(par, j, fixed, dinv[j] * r)

        rows_first(resid_row)
        halo_send(n + 1)
        rows_rest(resid_row)
        halo_sent(n + 1)

        n1 = n + 1
        par1 = lax.rem(n1, 2)
        halo_take(n1)

        def smooth_row(j, fixed):
            tbuf[j] = split(r_ref[j] - SMOOTH * product(par1, j))

        rows_first(smooth_row)
        rows_rest(smooth_row)

        def restrict(g, acc):
            for u in range(8):
                j = g * 8 + u
                acc = acc + lax.dot_general(
                    tbuf[j], table[j], (((1,), (1,)), ((), ())), preferred_element_type=F32
                )
            return acc

        acc = lax.fori_loop(0, nrows // 8, restrict, jnp.zeros((2 * nright, width), F32))
        right_one = (acc[:nright] + acc[nright:]) * scale_one

        fbuf[cyc, 4] = right_one
        for o in OFFSETS[:4]:
            coarse_copy(cyc, o).start()
        rate = {o: RELAX * small[o + 4, 0:1] for o in range(-4, 5)}
        rhs_one, it, parts = {}, {}, {}

        def first(o):
            rhs_one[o] = fbuf[cyc, o + 4]
            it[o] = rate[o] * rhs_one[o]
            parts[o] = split(it[o])

        def improve(offsets):
            return {
                o: it[o] + rate[o] * (rhs_one[o] - coarse_op(o, parts)) for o in offsets
            }

        first(0)
        for o in OFFSETS[:4]:
            coarse_copy(cyc, -o).wait_recv()
            first(o)
        second = improve((-1, 0, 1))
        resid_one = rhs_one[0] - coarse_op(0, {o: split(second[o]) for o in second})
        padded = jnp.concatenate([resid_one, jnp.zeros((width - nright, width), F32)], axis=0)
        tile = lax.dot_general(
            table_two, padded, (((1,), (1,)), ((), ())),
            precision=lax.Precision.HIGHEST, preferred_element_type=F32,
        )

        def send_far():
            for o in OFFSETS[4:]:
                coarse_copy(cyc, o).start()

        gather_all(cyc, tile, send_far)
        e2 = fold(jnp.dot(inv_s[...], gfull[...], preferred_element_type=F32), 56, width)
        e2t = split(
            jnp.concatenate([e2, jnp.zeros((width - 56, width), F32)], axis=0).T[:nright]
        )
        for o in OFFSETS[4:]:
            coarse_copy(cyc, -o).wait_recv()
            first(o)
        second.update(improve((-3, -2, 2, 3)))
        it = {
            o: second[o]
            + fold(jnp.dot(e2t, tw[o + 3], preferred_element_type=F32), nright, width)
            for o in second
        }
        parts = {o: split(it[o]) for o in it}
        it = improve((-2, -1, 0, 1, 2))
        parts = {o: split(it[o]) for o in it}
        it = improve((-1, 0, 1))
        for o in (-1, 0, 1):
            cx[o + 1] = split(it[o] * small[o + 4, 1:2])
        for o in OFFSETS:
            coarse_copy(cyc, o).wait_send()

        n2 = n + 2
        par2 = lax.rem(n2, 2)

        def lifted(value, hot):
            res = jnp.dot(value, hot, preferred_element_type=F32)
            return res[:nright] + res[nright:]

        def lift_row(j, fixed):
            u = lifted(cx[1], table[j])
            u_ref[j] = u
            publish(1 - par2, j, None, u)

        rows_first(lift_row)
        rows_rest(lift_row)
        for m in range(8):
            xs[par2, nrows + m] = split(lifted(cx[2 * (m // 4)], near_table[m]))

        def correct_row(j, fixed):
            d = SMOOTH * dinv[j]
            new = x_ref[j] + u_ref[j] - d * product(par2, j)
            x_ref[j] = new
            publish(par2, j, fixed, new)

        rows_first(correct_row)
        halo_send(n2 + 1)
        rows_rest(correct_row)
        halo_sent(n2 + 1)

        def sweeps(s, _):
            sweep(n2 + 1 + s, 12)
            return 0

        lax.fori_loop(0, 4 - 2 * cyc, sweeps, 0)
        return 0

    lax.fori_loop(0, 2, cycle, 0)
    for i in range(nrows):
        out_ref[:, i * width:(i + 1) * width] = x_ref[pos[i]]


def local(
    rhs_fields, diag_blocks, off_blocks, block_cols, send_lists, fine_agg,
    coarse_diag, coarse_side, coarse_agg, coarse_inverse,
):
    nrows, width = diag_blocks.shape[0], diag_blocks.shape[1]
    nright = rhs_fields.shape[0]
    naggs = coarse_diag.shape[1]
    S = pl.BlockSpec(memory_space=pltpu.SMEM)
    V = pl.BlockSpec(memory_space=pltpu.VMEM)
    A = pl.BlockSpec(memory_space=pl.ANY)
    DMA = pltpu.SemaphoreType.DMA
    return pl.pallas_call(
        kernel,
        name="multigrid",
        out_shape=jax.ShapeDtypeStruct(rhs_fields.shape, F32),
        in_specs=[S, S, A, A, A, V, V, V, V, A],
        out_specs=V,
        scratch_shapes=[
            pltpu.SMEM((nrows,), jnp.int32),
            pltpu.SMEM((nrows,), jnp.int32),
            pltpu.SMEM((3 * nrows,), jnp.int32),
            pltpu.SMEM((8,), jnp.int32),
            pltpu.VMEM(rhs_fields.shape, F32),
            pltpu.VMEM(diag_blocks.shape, F32),
            pltpu.VMEM(off_blocks.shape, F32),
            pltpu.VMEM((7, 8, coarse_inverse.shape[1]), F32),
            pltpu.VMEM((nrows, 4 * width, 2 * width), BF16),
            pltpu.VMEM((2, nrows + 8, 2 * nright, width), BF16),
            pltpu.VMEM((nrows, nright, width), F32),
            pltpu.VMEM((nrows, nright, width), F32),
            pltpu.VMEM((nrows, nright, width), F32),
            pltpu.VMEM((nrows, nright, width), F32),
            pltpu.VMEM((nrows, 1, width), F32),
            pltpu.VMEM((nrows, 1, width), F32),
            pltpu.VMEM((nrows, naggs, width), BF16),
            pltpu.VMEM((nrows, 2 * nright, width), BF16),
            pltpu.VMEM((8, nright, width), F32),
            pltpu.VMEM((3, 2, 4, nright, width), F32),
            pltpu.VMEM((3, 2, 4, nright, width), F32),
            pltpu.VMEM((7, 3 * width, 2 * width), BF16),
            pltpu.VMEM((3, 2 * nright, width), BF16),
            pltpu.VMEM((9, 16, width), F32),
            pltpu.VMEM((7, width, width), F32),
            pltpu.VMEM((7, 2, width, width), F32),
            pltpu.VMEM((2, 9, nright, width), F32),
            pltpu.VMEM((7, width, 2 * width), BF16),
            pltpu.VMEM((8, width, width), BF16),
            pltpu.VMEM((112, coarse_inverse.shape[1]), BF16),
            pltpu.VMEM((2, 2, 8, width), F32),
            pltpu.VMEM((2, 64, 8, width), F32),
            pltpu.VMEM((1024, 2 * width), BF16),
            DMA((9,)),
            DMA((nrows // CHUNK,)),
            DMA((3, 2)),
            DMA((3, 2)),
            DMA((9,)),
            DMA((9,)),
            DMA((2, 7)),
            DMA((2, 7)),
            DMA((2, 9)),
            DMA((2, 9)),
            DMA((2, 10)),
            DMA((2, 10)),
        ],
        compiler_params=pltpu.CompilerParams(
            collective_id=0, has_side_effects=True, vmem_limit_bytes=60 * 1024 * 1024
        ),
    )(
        block_cols.reshape(-1), send_lists.reshape(-1),
        rhs_fields, diag_blocks, off_blocks, fine_agg.reshape(nrows, 1, width),
        coarse_diag, coarse_side, coarse_agg.reshape(1, naggs), coarse_inverse,
    )


def solution(mesh):
    return jax.shard_map(
        local,
        mesh=mesh,
        in_specs=(
            P(None, "dom"),
            P("dom", None, None),
            P("dom", None, None, None),
            P("dom", None),
            P("dom", None, None),
            P("dom"),
            P("dom", None, None),
            P("dom", None, None, None),
            P("dom"),
            P(),
        ),
        out_specs=P(None, "dom"),
        check_vma=False,
    )
```

```python
import jax
import jax.numpy as jnp
from jax import lax
from jax.experimental import pallas as pl
from jax.experimental.pallas import tpu as pltpu
from jax.sharding import PartitionSpec as P

MESH = pl.DeviceIdType.MESH
RELAX = 0.6
SMOOTH = 0.5
F32 = jnp.float32
BF16 = jnp.bfloat16
CHUNK = 4
FIRST = 8
GROUP = 24
OFFSETS = (1, -1, 2, -2, 3, -3, 4, -4)


def split(x):
    hi = x.astype(BF16)
    lo = (x - hi.astype(F32)).astype(BF16)
    return jnp.concatenate([hi, lo], axis=0)


def split_columns(x):
    hi = x.astype(BF16)
    lo = (x - hi.astype(F32)).astype(BF16)
    return jnp.concatenate([hi, lo], axis=1)


def fold(res, rows, width):
    return res[:rows, :width] + res[:rows, width:] + res[rows:, :width]


def kernel(
    cols_in, lists_in,
    rhs_hbm, diag_hbm, off_hbm, agg_ref, cdiag_ref, cside_ref, cagg_ref, inv_hbm,
    out_ref,
    perm, pos, cols, sent_pos,
    rhs_v, diag_v, off_v, inv_v, weights, xs, x_ref, r_ref, u_ref, f_ref, dnat, dinv, table, tbuf,
    first8, send, recv, cw, cx, small, big_diag, big_side, fbuf, tw, near_table, inv_s,
    gtile, gather, gfull,
    load_sem, off_sem, send_sem, recv_sem, small_send, small_recv, big_send, big_recv,
    fsend_sem, frecv_sem, gsend_sem, grecv_sem,
):
    nright, nrows, width = f_ref.shape[1], f_ref.shape[0], f_ref.shape[2]
    me = lax.axis_index("dom")
    count = 128
    upper = lax.rem(me + 1, count)
    lower = lax.rem(me + count - 1, count)
    core = lax.rem(me, 2)
    y = lax.rem(me // 2, 4)
    z = lax.rem(me // 8, 4)
    xc = me // 32
    partner = me + 1 - 2 * core

    def member(ax, step):
        if ax == 0:
            return me + 2 * (lax.rem(y + step, 4) - y)
        if ax == 1:
            return me + 8 * (lax.rem(z + step, 4) - z)
        return me + 32 * (lax.rem(xc + step, 4) - xc)

    load_rhs = pltpu.make_async_copy(rhs_hbm, rhs_v, load_sem.at[0])
    load_diag = pltpu.make_async_copy(diag_hbm, diag_v, load_sem.at[1])
    def at_offset(o):
        return lax.rem(me + o + count, count)

    load_inv = [
        pltpu.make_async_copy(
            inv_hbm.at[pl.ds(pl.multiple_of(at_offset(o) * 8, 8), 8)],
            inv_v.at[o + 3], load_sem.at[5 + o],
        )
        for o in range(-3, 4)
    ]
    load_diag.start()
    load_rhs.start()

    def load_off(c):
        rows = pl.ds(c * CHUNK, CHUNK)
        return pltpu.make_async_copy(off_hbm.at[rows], off_v.at[rows], off_sem.at[c])

    for c in range(nrows // CHUNK):
        load_off(c).start()
    for load in load_inv:
        load.start()

    barrier = pltpu.get_barrier_semaphore()
    peers = [at_offset(o) for o in OFFSETS] + [member(ax, s) for ax in range(3) for s in (1, 2, 3)]
    for peer in peers:
        pl.semaphore_signal(barrier, inc=1, device_id=(peer,), device_id_type=MESH)

    wanted = [lists_in[m] for m in range(8)]

    def count_sent(i, total):
        flag = wanted[0] == i
        for m in range(1, 8):
            flag = jnp.logical_or(flag, wanted[m] == i)
        value = flag.astype(jnp.int32)
        pos[i] = value
        return total + value

    nsent = lax.fori_loop(0, nrows, count_sent, jnp.int32(0))

    def place(i, carry):
        a, b = carry
        value = pos[i]
        pos[i] = jnp.where(value == 1, a, b)
        return a + value, b + 1 - value

    lax.fori_loop(0, nrows, place, (jnp.int32(0), nsent))

    def invert(j, _):
        total = jnp.int32(0)
        for i in range(nrows):
            total = total + jnp.where(pos[i] == j, i, 0)
        perm[j] = total
        for k in range(3):
            c = cols_in[total * 3 + k]
            own = pos[jnp.minimum(c, nrows - 1)]
            cols[j * 3 + k] = jnp.where(c < nrows, own, c)
        return 0

    lax.fori_loop(0, nrows, invert, 0)
    for m in range(8):
        sent_pos[m] = pos[wanted[m]]

    def halo_copies(n):
        slot = lax.rem(n, 3)
        up = pltpu.make_async_remote_copy(
            src_ref=send.at[slot, 1], dst_ref=recv.at[slot, 0],
            send_sem=send_sem.at[slot, 1], recv_sem=recv_sem.at[slot, 0],
            device_id=(upper,), device_id_type=MESH,
        )
        down = pltpu.make_async_remote_copy(
            src_ref=send.at[slot, 0], dst_ref=recv.at[slot, 1],
            send_sem=send_sem.at[slot, 0], recv_sem=recv_sem.at[slot, 1],
            device_id=(lower,), device_id_type=MESH,
        )
        return up, down

    def halo_send(n):
        slot = lax.rem(n, 3)
        for m in range(8):
            send[slot, m // 4, m % 4] = first8[sent_pos[m]]
        up, down = halo_copies(n)
        up.start()
        down.start()

    def halo_sent(n):
        for copy in halo_copies(n):
            copy.wait_send()

    def halo_take(n):
        slot, par = lax.rem(n, 3), lax.rem(n, 2)
        for copy in halo_copies(n):
            copy.wait_recv()
        for m in range(8):
            xs[par, nrows + m] = split(recv[slot, m // 4, m % 4])

    def product(par, j):
        parts = [xs[par, j]] + [xs[par, cols[j * 3 + k]] for k in range(3)]
        res = jnp.dot(
            jnp.concatenate(parts, axis=1), weights[perm[j]], preferred_element_type=F32
        )
        return fold(res, nright, width)

    def rows_first(compute, store):
        for g in range(0, 8, FIRST):
            values = [compute(j) for j in range(g, g + FIRST)]
            for u in range(FIRST):
                store(g + u, g + u, values[u])

    def rows_rest(compute, store):
        def step(g, _):
            values = [compute(8 + g * GROUP + u) for u in range(GROUP)]
            for u in range(GROUP):
                store(8 + g * GROUP + u, None, values[u])
            return 0

        lax.fori_loop(0, (nrows - 8) // GROUP, step, 0)

    def publish(par, j, fixed, v):
        xs[1 - par, j] = split(v)
        if fixed is not None:
            first8[fixed] = v

    rows_iota = lax.broadcasted_iota(jnp.int32, (width, width), 0)
    eye = rows_iota == lax.broadcasted_iota(jnp.int32, (width, width), 1)
    load_diag.wait()

    def take_diag(i, _):
        d = jnp.sum(jnp.where(eye, diag_v[i], 0.0), axis=0, keepdims=True)
        dnat[i] = 1.0 / d
        return 0

    lax.fori_loop(0, nrows, take_diag, 0)
    load_rhs.wait()
    for i in range(nrows):
        u_ref[i] = rhs_v[:, i * width:(i + 1) * width]

    def start_load(j):
        return dnat[perm[j]], u_ref[perm[j]]

    def start_row(j, fixed, value):
        d, f = value
        dinv[j] = d
        f_ref[j] = f
        v = RELAX * d * f
        x_ref[j] = v
        publish(jnp.int32(1), j, fixed, v)

    rows_first(start_load, start_row)
    pl.semaphore_wait(barrier, len(peers))
    halo_send(jnp.int32(0))
    rows_rest(start_load, start_row)

    def big_copies(o):
        return [
            pltpu.make_async_remote_copy(
                src_ref=src, dst_ref=dst.at[3 - o],
                send_sem=big_send.at[i, 3 - o], recv_sem=big_recv.at[i, 3 - o],
                device_id=(at_offset(o),), device_id_type=MESH,
            )
            for i, (src, dst) in enumerate(
                [(cdiag_ref.at[0], big_diag), (cside_ref.at[0], big_side)]
            )
        ]

    for o in OFFSETS[:6]:
        for copy in big_copies(o):
            copy.start()

    def convert(c, _):
        load_off(c).wait()
        for q in range(CHUNK):
            i = c * CHUNK + q
            weights[i, 0:width] = split_columns(diag_v[i].T)
            for k in range(3):
                weights[i, (k + 1) * width:(k + 2) * width] = split_columns(off_v[i, k].T)
        return 0

    lax.fori_loop(0, nrows // CHUNK, convert, 0)

    def make_table(j, sums):
        hot = (agg_ref[perm[j]] == rows_iota).astype(F32)
        table[j] = hot.astype(BF16)
        return sums + hot

    sums = lax.fori_loop(0, nrows, make_table, jnp.zeros((width, width), F32))
    count_one = jnp.sum(sums, axis=1, keepdims=True)
    scale_one = (1.0 / jnp.sqrt(jnp.broadcast_to(count_one, (width, width)))).T[0:1]
    hot_two = (cagg_ref[...] == lax.broadcasted_iota(jnp.int32, (8, width), 0)).astype(F32)
    table_two = hot_two * (1.0 / jnp.sqrt(jnp.sum(hot_two, axis=1, keepdims=True)))
    cd = cdiag_ref[0]
    d1inv = 1.0 / jnp.sum(jnp.where(eye, cd, 0.0), axis=0, keepdims=True)
    lists = [agg_ref[wanted[m]].astype(F32) for m in range(8)]
    small[4] = jnp.concatenate(
        [d1inv, scale_one, cagg_ref[...].astype(F32), jnp.zeros((1, width), F32)]
        + lists + [jnp.zeros((4, width), F32)],
        axis=0,
    )

    def small_copy(o):
        return pltpu.make_async_remote_copy(
            src_ref=small.at[4], dst_ref=small.at[4 - o],
            send_sem=small_send.at[4 - o], recv_sem=small_recv.at[4 - o],
            device_id=(at_offset(o),), device_id_type=MESH,
        )

    for o in OFFSETS:
        small_copy(o).start()
    big_diag[3] = cd
    big_side[3] = cside_ref[0]
    for load in load_inv:
        load.wait()
    inv_s[...] = split(jnp.concatenate([inv_v[k] for k in range(7)], axis=0))
    float_rows = rows_iota.astype(F32)

    def take_near():
        for o in OFFSETS[:6]:
            for copy in big_copies(o):
                copy.wait()
        for o in OFFSETS:
            small_copy(o).wait()

        def weigh(k, _):
            cw[k, 0:width] = split_columns(big_diag[k].T)
            cw[k, width:2 * width] = split_columns(big_side[k, 0].T)
            cw[k, 2 * width:3 * width] = split_columns(big_side[k, 1].T)
            shift = (8 * k).astype(F32)
            hot = ((small[k + 1, 2:3] + shift) == float_rows).astype(F32)
            members = jnp.maximum(jnp.sum(hot, axis=1, keepdims=True), 1.0)
            tw[k] = split_columns(hot * (1.0 / jnp.sqrt(members)))
            return 0

        lax.fori_loop(0, 7, weigh, 0)
        for m in range(4):
            near_table[m] = (small[3, 8 + m:9 + m] == float_rows).astype(BF16)
            near_table[4 + m] = (small[5, 4 + m:5 + m] == float_rows).astype(BF16)

    def coarse_copy(cyc, o):
        return pltpu.make_async_remote_copy(
            src_ref=fbuf.at[cyc, 4], dst_ref=fbuf.at[cyc, 4 - o],
            send_sem=fsend_sem.at[cyc, 4 - o], recv_sem=frecv_sem.at[cyc, 4 - o],
            device_id=(at_offset(o),), device_id_type=MESH,
        )

    def coarse_op(o, parts):
        lhs = jnp.concatenate([parts[o], parts[o - 1], parts[o + 1]], axis=1)
        return fold(jnp.dot(lhs, cw[o + 3], preferred_element_type=F32), nright, width)

    chip = me // 2

    def gather_copies(cyc, ax):
        size = (1, 4, 16)[ax]
        first = (chip // size) * size
        out = []
        for s in (1, 2, 3):
            where = gather.at[cyc, pl.ds(first, size)]
            out.append(pltpu.make_async_remote_copy(
                src_ref=where, dst_ref=where,
                send_sem=gsend_sem.at[cyc, ax * 3 + s], recv_sem=grecv_sem.at[cyc, ax * 3 + s],
                device_id=(member(ax, s),), device_id_type=MESH,
            ))
        return out

    def gather_waits(cyc, ax):
        size = (1, 4, 16)[ax]
        for s in (1, 2, 3):
            source = member(ax, 4 - s) // 2
            where = gather.at[cyc, pl.ds((source // size) * size, size)]
            pltpu.make_async_remote_copy(
                src_ref=where, dst_ref=where,
                send_sem=gsend_sem.at[cyc, ax * 3 + s], recv_sem=grecv_sem.at[cyc, ax * 3 + s],
                device_id=(member(ax, s),), device_id_type=MESH,
            ).wait_recv()

    def gather_all(cyc, tile, between):
        gtile[cyc, 0] = tile
        pair = pltpu.make_async_remote_copy(
            src_ref=gtile.at[cyc, 0], dst_ref=gtile.at[cyc, 1],
            send_sem=gsend_sem.at[cyc, 0], recv_sem=grecv_sem.at[cyc, 0],
            device_id=(partner,), device_id_type=MESH,
        )
        pair.start()
        pair.wait()
        other = gtile[cyc, 1]
        even = jnp.where(core == 0, tile, other)
        odd = jnp.where(core == 0, other, tile)
        low_lanes = lax.broadcasted_iota(jnp.int32, (8, width), 1) < nright
        gather[cyc, pl.ds(chip, 1)] = jnp.where(low_lanes, even, pltpu.roll(odd, nright, 1))[None]
        for ax in range(3):
            copies = gather_copies(cyc, ax)
            for copy in copies:
                copy.start()
            gather_waits(cyc, ax)
            for copy in copies:
                copy.wait_send()
            if ax == 0:
                between()
        for c in range(64):
            pair_tile = gather[cyc, c]
            gfull[16 * c:16 * c + 8] = split_columns(pair_tile)
            gfull[16 * c + 8:16 * c + 16] = split_columns(pltpu.roll(pair_tile, nright, 1))

    def sweep(n, last):
        par = lax.rem(n, 2)
        halo_take(n)

        def relax(j):
            d = RELAX * dinv[j]
            return x_ref[j] + d * (f_ref[j] - product(par, j))

        def body(j, fixed, new):
            x_ref[j] = new
            publish(par, j, fixed, new)

        rows_first(relax, body)
        if last is None:
            halo_send(n + 1)
        else:
            @pl.when(n < last)
            def _():
                halo_send(n + 1)
        rows_rest(relax, body)
        if last is None:
            halo_sent(n + 1)
        else:
            @pl.when(n < last)
            def _():
                halo_sent(n + 1)

    halo_sent(jnp.int32(0))
    sweep(jnp.int32(0), None)
    take_near()

    def cycle(cyc, _):
        n = 1 + 7 * cyc
        par = lax.rem(n, 2)
        halo_take(n)

        def resid(j):
            return f_ref[j] - product(par, j)

        def resid_row(j, fixed, r):
            r_ref[j] = r
            publish(par, j, fixed, dinv[j] * r)

        rows_first(resid, resid_row)
        halo_send(n + 1)
        rows_rest(resid, resid_row)
        halo_sent(n + 1)

        n1 = n + 1
        par1 = lax.rem(n1, 2)
        halo_take(n1)

        def smooth(j):
            return r_ref[j] - SMOOTH * product(par1, j)

        def smooth_row(j, fixed, t):
            tbuf[j] = split(t)

        rows_first(smooth, smooth_row)
        rows_rest(smooth, smooth_row)

        def restrict(g, acc):
            for u in range(8):
                j = g * 8 + u
                acc = acc + lax.dot_general(
                    tbuf[j], table[j], (((1,), (1,)), ((), ())), preferred_element_type=F32
                )
            return acc

        acc = lax.fori_loop(0, nrows // 8, restrict, jnp.zeros((2 * nright, width), F32))
        right_one = (acc[:nright] + acc[nright:]) * scale_one

        fbuf[cyc, 4] = right_one
        for o in OFFSETS[:4]:
            coarse_copy(cyc, o).start()
        rate = {o: RELAX * small[o + 4, 0:1] for o in range(-4, 5)}
        rhs_one, it, parts = {}, {}, {}

        def first(o):
            rhs_one[o] = fbuf[cyc, o + 4]
            it[o] = rate[o] * rhs_one[o]
            parts[o] = split(it[o])

        def improve(offsets):
            return {
                o: it[o] + rate[o] * (rhs_one[o] - coarse_op(o, parts)) for o in offsets
            }

        first(0)
        for o in OFFSETS[:4]:
            coarse_copy(cyc, -o).wait_recv()
            first(o)
        second = improve((-1, 0, 1))
        resid_one = rhs_one[0] - coarse_op(0, {o: split(second[o]) for o in second})
        padded = jnp.concatenate([resid_one, jnp.zeros((width - nright, width), F32)], axis=0)
        tile = lax.dot_general(
            table_two, padded, (((1,), (1,)), ((), ())),
            precision=lax.Precision.HIGHEST, preferred_element_type=F32,
        )

        def send_far():
            for o in OFFSETS[4:]:
                coarse_copy(cyc, o).start()

        gather_all(cyc, tile, send_far)
        e2 = fold(jnp.dot(inv_s[...], gfull[...], preferred_element_type=F32), 56, width)
        e2t = split(
            jnp.concatenate([e2, jnp.zeros((width - 56, width), F32)], axis=0).T[:nright]
        )
        for o in OFFSETS[4:]:
            coarse_copy(cyc, -o).wait_recv()
            first(o)
        second.update(improve((-3, -2, 2, 3)))
        it = {
            o: second[o]
            + fold(jnp.dot(e2t, tw[o + 3], preferred_element_type=F32), nright, width)
            for o in second
        }
        parts = {o: split(it[o]) for o in it}
        it = improve((-2, -1, 0, 1, 2))
        parts = {o: split(it[o]) for o in it}
        it = improve((-1, 0, 1))
        for o in (-1, 0, 1):
            cx[o + 1] = split(it[o] * small[o + 4, 1:2])
        for o in OFFSETS:
            coarse_copy(cyc, o).wait_send()

        n2 = n + 2
        par2 = lax.rem(n2, 2)

        def lifted(value, hot):
            res = jnp.dot(value, hot, preferred_element_type=F32)
            return res[:nright] + res[nright:]

        def lift(j):
            return lifted(cx[1], table[j])

        def lift_row(j, fixed, u):
            u_ref[j] = u
            publish(1 - par2, j, None, u)

        rows_first(lift, lift_row)
        rows_rest(lift, lift_row)
        for m in range(8):
            xs[par2, nrows + m] = split(lifted(cx[2 * (m // 4)], near_table[m]))

        def correct(j):
            d = SMOOTH * dinv[j]
            return x_ref[j] + u_ref[j] - d * product(par2, j)

        def correct_row(j, fixed, new):
            x_ref[j] = new
            publish(par2, j, fixed, new)

        rows_first(correct, correct_row)
        halo_send(n2 + 1)
        rows_rest(correct, correct_row)
        halo_sent(n2 + 1)

        def sweeps(s, _):
            sweep(n2 + 1 + s, 12)
            return 0

        lax.fori_loop(0, 4 - 2 * cyc, sweeps, 0)
        return 0

    lax.fori_loop(0, 2, cycle, 0)
    for i in range(nrows):
        out_ref[:, i * width:(i + 1) * width] = x_ref[pos[i]]


def local(
    rhs_fields, diag_blocks, off_blocks, block_cols, send_lists, fine_agg,
    coarse_diag, coarse_side, coarse_agg, coarse_inverse,
):
    nrows, width = diag_blocks.shape[0], diag_blocks.shape[1]
    nright = rhs_fields.shape[0]
    naggs = coarse_diag.shape[1]
    S = pl.BlockSpec(memory_space=pltpu.SMEM)
    V = pl.BlockSpec(memory_space=pltpu.VMEM)
    A = pl.BlockSpec(memory_space=pl.ANY)
    DMA = pltpu.SemaphoreType.DMA
    return pl.pallas_call(
        kernel,
        name="multigrid",
        out_shape=jax.ShapeDtypeStruct(rhs_fields.shape, F32),
        in_specs=[S, S, A, A, A, V, V, V, V, A],
        out_specs=V,
        scratch_shapes=[
            pltpu.SMEM((nrows,), jnp.int32),
            pltpu.SMEM((nrows,), jnp.int32),
            pltpu.SMEM((3 * nrows,), jnp.int32),
            pltpu.SMEM((8,), jnp.int32),
            pltpu.VMEM(rhs_fields.shape, F32),
            pltpu.VMEM(diag_blocks.shape, F32),
            pltpu.VMEM(off_blocks.shape, F32),
            pltpu.VMEM((7, 8, coarse_inverse.shape[1]), F32),
            pltpu.VMEM((nrows, 4 * width, 2 * width), BF16),
            pltpu.VMEM((2, nrows + 8, 2 * nright, width), BF16),
            pltpu.VMEM((nrows, nright, width), F32),
            pltpu.VMEM((nrows, nright, width), F32),
            pltpu.VMEM((nrows, nright, width), F32),
            pltpu.VMEM((nrows, nright, width), F32),
            pltpu.VMEM((nrows, 1, width), F32),
            pltpu.VMEM((nrows, 1, width), F32),
            pltpu.VMEM((nrows, naggs, width), BF16),
            pltpu.VMEM((nrows, 2 * nright, width), BF16),
            pltpu.VMEM((8, nright, width), F32),
            pltpu.VMEM((3, 2, 4, nright, width), F32),
            pltpu.VMEM((3, 2, 4, nright, width), F32),
            pltpu.VMEM((7, 3 * width, 2 * width), BF16),
            pltpu.VMEM((3, 2 * nright, width), BF16),
            pltpu.VMEM((9, 16, width), F32),
            pltpu.VMEM((7, width, width), F32),
            pltpu.VMEM((7, 2, width, width), F32),
            pltpu.VMEM((2, 9, nright, width), F32),
            pltpu.VMEM((7, width, 2 * width), BF16),
            pltpu.VMEM((8, width, width), BF16),
            pltpu.VMEM((112, coarse_inverse.shape[1]), BF16),
            pltpu.VMEM((2, 2, 8, width), F32),
            pltpu.VMEM((2, 64, 8, width), F32),
            pltpu.VMEM((1024, 2 * width), BF16),
            DMA((9,)),
            DMA((nrows // CHUNK,)),
            DMA((3, 2)),
            DMA((3, 2)),
            DMA((9,)),
            DMA((9,)),
            DMA((2, 7)),
            DMA((2, 7)),
            DMA((2, 9)),
            DMA((2, 9)),
            DMA((2, 10)),
            DMA((2, 10)),
        ],
        compiler_params=pltpu.CompilerParams(
            collective_id=0, has_side_effects=True, vmem_limit_bytes=60 * 1024 * 1024
        ),
    )(
        block_cols.reshape(-1), send_lists.reshape(-1),
        rhs_fields, diag_blocks, off_blocks, fine_agg.reshape(nrows, 1, width),
        coarse_diag, coarse_side, coarse_agg.reshape(1, naggs), coarse_inverse,
    )


def solution(mesh):
    return jax.shard_map(
        local,
        mesh=mesh,
        in_specs=(
            P(None, "dom"),
            P("dom", None, None),
            P("dom", None, None, None),
            P("dom", None),
            P("dom", None, None),
            P("dom"),
            P("dom", None, None),
            P("dom", None, None, None),
            P("dom"),
            P(),
        ),
        out_specs=P(None, "dom"),
        check_vma=False,
    )
```

```python
import jax
import jax.numpy as jnp
from jax import lax
from jax.experimental import pallas as pl
from jax.experimental.pallas import tpu as pltpu
from jax.sharding import PartitionSpec as P

MESH = pl.DeviceIdType.MESH
RELAX = 0.6
SMOOTH = 0.5
F32 = jnp.float32
BF16 = jnp.bfloat16
CHUNK = 4
GROUP = 16
OFFSETS = (1, -1, 2, -2, 3, -3, 4, -4)


def split(x):
    hi = x.astype(BF16)
    lo = (x - hi.astype(F32)).astype(BF16)
    return jnp.concatenate([hi, lo], axis=0)


def split_columns(x):
    hi = x.astype(BF16)
    lo = (x - hi.astype(F32)).astype(BF16)
    return jnp.concatenate([hi, lo], axis=1)


def fold(res, rows, width):
    return res[:rows, :width] + res[:rows, width:] + res[rows:, :width]


def kernel(
    cols_in, lists_in,
    rhs_hbm, diag_hbm, off_hbm, agg_ref, cdiag_ref, cside_ref, cagg_ref, inv_hbm,
    out_ref,
    rhs_v, diag_v, off_v, inv_v, weights, xs, x_ref, r_ref, u_ref, f_ref, dinv, table, tbuf,
    send, recv, cw, cx, small, big_diag, big_side, fbuf, tw, near_table, inv_s,
    gtile, gather, gfull,
    load_sem, off_sem, send_sem, recv_sem, small_send, small_recv, big_send, big_recv,
    fsend_sem, frecv_sem, gsend_sem, grecv_sem,
):
    nright, nrows, width = f_ref.shape[1], f_ref.shape[0], f_ref.shape[2]
    me = lax.axis_index("dom")
    count = 128
    upper = lax.rem(me + 1, count)
    lower = lax.rem(me + count - 1, count)
    core = lax.rem(me, 2)
    y = lax.rem(me // 2, 4)
    z = lax.rem(me // 8, 4)
    xc = me // 32
    partner = me + 1 - 2 * core

    def member(ax, step):
        if ax == 0:
            return me + 2 * (lax.rem(y + step, 4) - y)
        if ax == 1:
            return me + 8 * (lax.rem(z + step, 4) - z)
        return me + 32 * (lax.rem(xc + step, 4) - xc)

    load_rhs = pltpu.make_async_copy(rhs_hbm, rhs_v, load_sem.at[0])
    load_diag = pltpu.make_async_copy(diag_hbm, diag_v, load_sem.at[1])
    def at_offset(o):
        return lax.rem(me + o + count, count)

    load_inv = [
        pltpu.make_async_copy(
            inv_hbm.at[pl.ds(pl.multiple_of(at_offset(o) * 8, 8), 8)],
            inv_v.at[o + 3], load_sem.at[5 + o],
        )
        for o in range(-3, 4)
    ]
    load_diag.start()
    load_rhs.start()

    def load_off(c):
        rows = pl.ds(c * CHUNK, CHUNK)
        return pltpu.make_async_copy(off_hbm.at[rows], off_v.at[rows], off_sem.at[c])

    for c in range(nrows // CHUNK):
        load_off(c).start()
    for load in load_inv:
        load.start()

    barrier = pltpu.get_barrier_semaphore()
    peers = [at_offset(o) for o in OFFSETS] + [member(ax, s) for ax in range(3) for s in (1, 2, 3)]
    for peer in peers:
        pl.semaphore_signal(barrier, inc=1, device_id=(peer,), device_id_type=MESH)

    wanted = [lists_in[m] for m in range(8)]

    def halo_copies(n, h):
        slot = lax.rem(n, 3)
        half = pl.ds(2 * h, 2)
        up = pltpu.make_async_remote_copy(
            src_ref=send.at[slot, 1, half], dst_ref=recv.at[slot, 0, half],
            send_sem=send_sem.at[slot, 1, h], recv_sem=recv_sem.at[slot, 0, h],
            device_id=(upper,), device_id_type=MESH,
        )
        down = pltpu.make_async_remote_copy(
            src_ref=send.at[slot, 0, half], dst_ref=recv.at[slot, 1, half],
            send_sem=send_sem.at[slot, 0, h], recv_sem=recv_sem.at[slot, 1, h],
            device_id=(lower,), device_id_type=MESH,
        )
        return up, down

    def halo_send(n, value):
        slot = lax.rem(n, 3)
        for h in range(2):
            places = [(side, 2 * h + q) for q in range(2) for side in range(2)]
            values = [value(wanted[4 * side + q]) for side, q in places]
            for (side, q), v in zip(places, values):
                send[slot, side, q] = v
            for copy in halo_copies(n, h):
                copy.start()

    def halo_sent(n):
        for h in range(2):
            for copy in halo_copies(n, h):
                copy.wait_send()

    def halo_take(n):
        slot, par = lax.rem(n, 3), lax.rem(n, 2)
        for h in range(2):
            for copy in halo_copies(n, h):
                copy.wait_recv()
            for q in range(2 * h, 2 * h + 2):
                for side in range(2):
                    xs[par, nrows + 4 * side + q] = split(recv[slot, side, q])

    def product(par, j):
        parts = [xs[par, j]] + [xs[par, cols_in[j * 3 + k]] for k in range(3)]
        res = jnp.dot(
            jnp.concatenate(parts, axis=1), weights[j], preferred_element_type=F32
        )
        return fold(res, nright, width)

    def rows(compute, store):
        def step(g, _):
            values = [compute(g * GROUP + u) for u in range(GROUP)]
            for u in range(GROUP):
                store(g * GROUP + u, values[u])
            return 0

        lax.fori_loop(0, nrows // GROUP, step, 0)

    def publish(par, j, v):
        xs[1 - par, j] = split(v)

    rows_iota = lax.broadcasted_iota(jnp.int32, (width, width), 0)
    eye = rows_iota == lax.broadcasted_iota(jnp.int32, (width, width), 1)
    load_diag.wait()

    def take_diag(i, _):
        d = jnp.sum(jnp.where(eye, diag_v[i], 0.0), axis=0, keepdims=True)
        dinv[i] = 1.0 / d
        return 0

    lax.fori_loop(0, nrows, take_diag, 0)
    load_rhs.wait()
    for i in range(nrows):
        f_ref[i] = rhs_v[:, i * width:(i + 1) * width]

    pl.semaphore_wait(barrier, len(peers))
    halo_send(jnp.int32(0), lambda q: RELAX * dinv[q] * f_ref[q])

    def start_row(j, v):
        x_ref[j] = v
        publish(jnp.int32(1), j, v)

    rows(lambda j: RELAX * dinv[j] * f_ref[j], start_row)

    def big_copies(o):
        return [
            pltpu.make_async_remote_copy(
                src_ref=src, dst_ref=dst.at[3 - o],
                send_sem=big_send.at[i, 3 - o], recv_sem=big_recv.at[i, 3 - o],
                device_id=(at_offset(o),), device_id_type=MESH,
            )
            for i, (src, dst) in enumerate(
                [(cdiag_ref.at[0], big_diag), (cside_ref.at[0], big_side)]
            )
        ]

    for o in OFFSETS[:6]:
        for copy in big_copies(o):
            copy.start()

    def convert(c, _):
        load_off(c).wait()
        for q in range(CHUNK):
            i = c * CHUNK + q
            weights[i, 0:width] = split_columns(diag_v[i].T)
            for k in range(3):
                weights[i, (k + 1) * width:(k + 2) * width] = split_columns(off_v[i, k].T)
        return 0

    lax.fori_loop(0, nrows // CHUNK, convert, 0)

    def make_table(j, sums):
        hot = (agg_ref[j] == rows_iota).astype(F32)
        table[j] = hot.astype(BF16)
        return sums + hot

    sums = lax.fori_loop(0, nrows, make_table, jnp.zeros((width, width), F32))
    count_one = jnp.sum(sums, axis=1, keepdims=True)
    scale_one = (1.0 / jnp.sqrt(jnp.broadcast_to(count_one, (width, width)))).T[0:1]
    hot_two = (cagg_ref[...] == lax.broadcasted_iota(jnp.int32, (8, width), 0)).astype(F32)
    table_two = hot_two * (1.0 / jnp.sqrt(jnp.sum(hot_two, axis=1, keepdims=True)))
    cd = cdiag_ref[0]
    d1inv = 1.0 / jnp.sum(jnp.where(eye, cd, 0.0), axis=0, keepdims=True)
    lists = [agg_ref[wanted[m]].astype(F32) for m in range(8)]
    small[4] = jnp.concatenate(
        [d1inv, scale_one, cagg_ref[...].astype(F32), jnp.zeros((1, width), F32)]
        + lists + [jnp.zeros((4, width), F32)],
        axis=0,
    )

    def small_copy(o):
        return pltpu.make_async_remote_copy(
            src_ref=small.at[4], dst_ref=small.at[4 - o],
            send_sem=small_send.at[4 - o], recv_sem=small_recv.at[4 - o],
            device_id=(at_offset(o),), device_id_type=MESH,
        )

    for o in OFFSETS:
        small_copy(o).start()
    big_diag[3] = cd
    big_side[3] = cside_ref[0]
    for load in load_inv:
        load.wait()
    inv_s[...] = split(jnp.concatenate([inv_v[k] for k in range(7)], axis=0))
    float_rows = rows_iota.astype(F32)

    def take_near():
        for o in OFFSETS[:6]:
            for copy in big_copies(o):
                copy.wait()
        for o in OFFSETS:
            small_copy(o).wait()

        def weigh(k, _):
            cw[k, 0:width] = split_columns(big_diag[k].T)
            cw[k, width:2 * width] = split_columns(big_side[k, 0].T)
            cw[k, 2 * width:3 * width] = split_columns(big_side[k, 1].T)
            shift = (8 * k).astype(F32)
            hot = ((small[k + 1, 2:3] + shift) == float_rows).astype(F32)
            members = jnp.maximum(jnp.sum(hot, axis=1, keepdims=True), 1.0)
            tw[k] = split_columns(hot * (1.0 / jnp.sqrt(members)))
            return 0

        lax.fori_loop(0, 7, weigh, 0)
        for m in range(4):
            near_table[m] = (small[3, 8 + m:9 + m] == float_rows).astype(BF16)
            near_table[4 + m] = (small[5, 4 + m:5 + m] == float_rows).astype(BF16)

    def coarse_copy(cyc, o):
        return pltpu.make_async_remote_copy(
            src_ref=fbuf.at[cyc, 4], dst_ref=fbuf.at[cyc, 4 - o],
            send_sem=fsend_sem.at[cyc, 4 - o], recv_sem=frecv_sem.at[cyc, 4 - o],
            device_id=(at_offset(o),), device_id_type=MESH,
        )

    def coarse_op(o, parts):
        lhs = jnp.concatenate([parts[o], parts[o - 1], parts[o + 1]], axis=1)
        return fold(jnp.dot(lhs, cw[o + 3], preferred_element_type=F32), nright, width)

    chip = me // 2

    def gather_copies(cyc, ax):
        size = (1, 4, 16)[ax]
        first = (chip // size) * size
        out = []
        for s in (1, 2, 3):
            where = gather.at[cyc, pl.ds(first, size)]
            out.append(pltpu.make_async_remote_copy(
                src_ref=where, dst_ref=where,
                send_sem=gsend_sem.at[cyc, ax * 3 + s], recv_sem=grecv_sem.at[cyc, ax * 3 + s],
                device_id=(member(ax, s),), device_id_type=MESH,
            ))
        return out

    def gather_waits(cyc, ax):
        size = (1, 4, 16)[ax]
        for s in (1, 2, 3):
            source = member(ax, 4 - s) // 2
            where = gather.at[cyc, pl.ds((source // size) * size, size)]
            pltpu.make_async_remote_copy(
                src_ref=where, dst_ref=where,
                send_sem=gsend_sem.at[cyc, ax * 3 + s], recv_sem=grecv_sem.at[cyc, ax * 3 + s],
                device_id=(member(ax, s),), device_id_type=MESH,
            ).wait_recv()

    def gather_all(cyc, tile, between):
        gtile[cyc, 0] = tile
        pair = pltpu.make_async_remote_copy(
            src_ref=gtile.at[cyc, 0], dst_ref=gtile.at[cyc, 1],
            send_sem=gsend_sem.at[cyc, 0], recv_sem=grecv_sem.at[cyc, 0],
            device_id=(partner,), device_id_type=MESH,
        )
        pair.start()
        pair.wait()
        other = gtile[cyc, 1]
        even = jnp.where(core == 0, tile, other)
        odd = jnp.where(core == 0, other, tile)
        low_lanes = lax.broadcasted_iota(jnp.int32, (8, width), 1) < nright
        gather[cyc, pl.ds(chip, 1)] = jnp.where(low_lanes, even, pltpu.roll(odd, nright, 1))[None]
        for ax in range(3):
            copies = gather_copies(cyc, ax)
            for copy in copies:
                copy.start()
            gather_waits(cyc, ax)
            for copy in copies:
                copy.wait_send()
            if ax == 0:
                between()
        for c in range(64):
            pair_tile = gather[cyc, c]
            gfull[16 * c:16 * c + 8] = split_columns(pair_tile)
            gfull[16 * c + 8:16 * c + 16] = split_columns(pltpu.roll(pair_tile, nright, 1))

    def sweep(n, last):
        par = lax.rem(n, 2)
        halo_take(n)

        def relax(j):
            d = RELAX * dinv[j]
            return x_ref[j] + d * (f_ref[j] - product(par, j))

        def body(j, new):
            x_ref[j] = new
            publish(par, j, new)

        if last is None:
            halo_send(n + 1, relax)
        else:
            @pl.when(n < last)
            def _():
                halo_send(n + 1, relax)
        rows(relax, body)
        if last is None:
            halo_sent(n + 1)
        else:
            @pl.when(n < last)
            def _():
                halo_sent(n + 1)

    halo_sent(jnp.int32(0))
    sweep(jnp.int32(0), None)
    take_near()

    def cycle(cyc, _):
        n = 1 + 7 * cyc
        par = lax.rem(n, 2)
        halo_take(n)

        def resid(j):
            return f_ref[j] - product(par, j)

        def resid_row(j, r):
            r_ref[j] = r
            publish(par, j, dinv[j] * r)

        halo_send(n + 1, lambda q: dinv[q] * resid(q))
        rows(resid, resid_row)
        halo_sent(n + 1)

        n1 = n + 1
        par1 = lax.rem(n1, 2)
        halo_take(n1)

        def smooth(j):
            return r_ref[j] - SMOOTH * product(par1, j)

        def smooth_row(j, t):
            tbuf[j] = split(t)

        rows(smooth, smooth_row)

        def restrict(g, acc):
            for u in range(8):
                j = g * 8 + u
                acc = acc + lax.dot_general(
                    tbuf[j], table[j], (((1,), (1,)), ((), ())), preferred_element_type=F32
                )
            return acc

        acc = lax.fori_loop(0, nrows // 8, restrict, jnp.zeros((2 * nright, width), F32))
        right_one = (acc[:nright] + acc[nright:]) * scale_one

        fbuf[cyc, 4] = right_one
        for o in OFFSETS[:4]:
            coarse_copy(cyc, o).start()
        rate = {o: RELAX * small[o + 4, 0:1] for o in range(-4, 5)}
        rhs_one, it, parts = {}, {}, {}

        def first(o):
            rhs_one[o] = fbuf[cyc, o + 4]
            it[o] = rate[o] * rhs_one[o]
            parts[o] = split(it[o])

        def improve(offsets):
            return {
                o: it[o] + rate[o] * (rhs_one[o] - coarse_op(o, parts)) for o in offsets
            }

        first(0)
        for o in OFFSETS[:4]:
            coarse_copy(cyc, -o).wait_recv()
            first(o)
        second = improve((-1, 0, 1))
        resid_one = rhs_one[0] - coarse_op(0, {o: split(second[o]) for o in second})
        padded = jnp.concatenate([resid_one, jnp.zeros((width - nright, width), F32)], axis=0)
        tile = lax.dot_general(
            table_two, padded, (((1,), (1,)), ((), ())),
            precision=lax.Precision.HIGHEST, preferred_element_type=F32,
        )

        def send_far():
            for o in OFFSETS[4:]:
                coarse_copy(cyc, o).start()

        gather_all(cyc, tile, send_far)
        e2 = fold(jnp.dot(inv_s[...], gfull[...], preferred_element_type=F32), 56, width)
        e2t = split(
            jnp.concatenate([e2, jnp.zeros((width - 56, width), F32)], axis=0).T[:nright]
        )
        for o in OFFSETS[4:]:
            coarse_copy(cyc, -o).wait_recv()
            first(o)
        second.update(improve((-3, -2, 2, 3)))
        it = {
            o: second[o]
            + fold(jnp.dot(e2t, tw[o + 3], preferred_element_type=F32), nright, width)
            for o in second
        }
        parts = {o: split(it[o]) for o in it}
        it = improve((-2, -1, 0, 1, 2))
        parts = {o: split(it[o]) for o in it}
        it = improve((-1, 0, 1))
        for o in (-1, 0, 1):
            cx[o + 1] = split(it[o] * small[o + 4, 1:2])
        for o in OFFSETS:
            coarse_copy(cyc, o).wait_send()

        n2 = n + 2
        par2 = lax.rem(n2, 2)

        def lifted(value, hot):
            res = jnp.dot(value, hot, preferred_element_type=F32)
            return res[:nright] + res[nright:]

        def lift(j):
            return lifted(cx[1], table[j])

        def lift_row(j, u):
            u_ref[j] = u
            publish(1 - par2, j, u)

        rows(lift, lift_row)
        for m in range(8):
            xs[par2, nrows + m] = split(lifted(cx[2 * (m // 4)], near_table[m]))

        def correct(j):
            d = SMOOTH * dinv[j]
            return x_ref[j] + u_ref[j] - d * product(par2, j)

        def correct_row(j, new):
            x_ref[j] = new
            publish(par2, j, new)

        halo_send(n2 + 1, correct)
        rows(correct, correct_row)
        halo_sent(n2 + 1)

        def sweeps(s, _):
            sweep(n2 + 1 + s, 12)
            return 0

        lax.fori_loop(0, 4 - 2 * cyc, sweeps, 0)
        return 0

    lax.fori_loop(0, 2, cycle, 0)
    for i in range(nrows):
        out_ref[:, i * width:(i + 1) * width] = x_ref[i]


def local(
    rhs_fields, diag_blocks, off_blocks, block_cols, send_lists, fine_agg,
    coarse_diag, coarse_side, coarse_agg, coarse_inverse,
):
    nrows, width = diag_blocks.shape[0], diag_blocks.shape[1]
    nright = rhs_fields.shape[0]
    naggs = coarse_diag.shape[1]
    S = pl.BlockSpec(memory_space=pltpu.SMEM)
    V = pl.BlockSpec(memory_space=pltpu.VMEM)
    A = pl.BlockSpec(memory_space=pl.ANY)
    DMA = pltpu.SemaphoreType.DMA
    return pl.pallas_call(
        kernel,
        name="multigrid",
        out_shape=jax.ShapeDtypeStruct(rhs_fields.shape, F32),
        in_specs=[S, S, A, A, A, V, V, V, V, A],
        out_specs=V,
        scratch_shapes=[
            pltpu.VMEM(rhs_fields.shape, F32),
            pltpu.VMEM(diag_blocks.shape, F32),
            pltpu.VMEM(off_blocks.shape, F32),
            pltpu.VMEM((7, 8, coarse_inverse.shape[1]), F32),
            pltpu.VMEM((nrows, 4 * width, 2 * width), BF16),
            pltpu.VMEM((2, nrows + 8, 2 * nright, width), BF16),
            pltpu.VMEM((nrows, nright, width), F32),
            pltpu.VMEM((nrows, nright, width), F32),
            pltpu.VMEM((nrows, nright, width), F32),
            pltpu.VMEM((nrows, nright, width), F32),
            pltpu.VMEM((nrows, 1, width), F32),
            pltpu.VMEM((nrows, naggs, width), BF16),
            pltpu.VMEM((nrows, 2 * nright, width), BF16),
            pltpu.VMEM((3, 2, 4, nright, width), F32),
            pltpu.VMEM((3, 2, 4, nright, width), F32),
            pltpu.VMEM((7, 3 * width, 2 * width), BF16),
            pltpu.VMEM((3, 2 * nright, width), BF16),
            pltpu.VMEM((9, 16, width), F32),
            pltpu.VMEM((7, width, width), F32),
            pltpu.VMEM((7, 2, width, width), F32),
            pltpu.VMEM((2, 9, nright, width), F32),
            pltpu.VMEM((7, width, 2 * width), BF16),
            pltpu.VMEM((8, width, width), BF16),
            pltpu.VMEM((112, coarse_inverse.shape[1]), BF16),
            pltpu.VMEM((2, 2, 8, width), F32),
            pltpu.VMEM((2, 64, 8, width), F32),
            pltpu.VMEM((1024, 2 * width), BF16),
            DMA((9,)),
            DMA((nrows // CHUNK,)),
            DMA((3, 2, 2)),
            DMA((3, 2, 2)),
            DMA((9,)),
            DMA((9,)),
            DMA((2, 7)),
            DMA((2, 7)),
            DMA((2, 9)),
            DMA((2, 9)),
            DMA((2, 10)),
            DMA((2, 10)),
        ],
        compiler_params=pltpu.CompilerParams(
            collective_id=0, has_side_effects=True, vmem_limit_bytes=60 * 1024 * 1024
        ),
    )(
        block_cols.reshape(-1), send_lists.reshape(-1),
        rhs_fields, diag_blocks, off_blocks, fine_agg.reshape(nrows, 1, width),
        coarse_diag, coarse_side, coarse_agg.reshape(1, naggs), coarse_inverse,
    )


def solution(mesh):
    return jax.shard_map(
        local,
        mesh=mesh,
        in_specs=(
            P(None, "dom"),
            P("dom", None, None),
            P("dom", None, None, None),
            P("dom", None),
            P("dom", None, None),
            P("dom"),
            P("dom", None, None),
            P("dom", None, None, None),
            P("dom"),
            P(),
        ),
        out_specs=P(None, "dom"),
        check_vma=False,
    )
```

```python
import jax
import jax.numpy as jnp
from jax import lax
from jax.experimental import pallas as pl
from jax.experimental.pallas import tpu as pltpu
from jax.sharding import PartitionSpec as P

MESH = pl.DeviceIdType.MESH
RELAX = 0.6
SMOOTH = 0.5
F32 = jnp.float32
BF16 = jnp.bfloat16
CHUNK = 4
GROUP = 32
OFFSETS = (1, -1, 2, -2, 3, -3, 4, -4)


def split(x):
    hi = x.astype(BF16)
    lo = (x - hi.astype(F32)).astype(BF16)
    return jnp.concatenate([hi, lo], axis=0)


def split_columns(x):
    hi = x.astype(BF16)
    lo = (x - hi.astype(F32)).astype(BF16)
    return jnp.concatenate([hi, lo], axis=1)


def fold(res, rows, width):
    return res[:rows, :width] + res[:rows, width:] + res[rows:, :width]


def kernel(
    cols_in, lists_in,
    rhs_hbm, diag_hbm, off_hbm, agg_ref, cdiag_ref, cside_ref, cagg_ref, inv_hbm,
    out_ref,
    rhs_v, diag_v, off_v, inv_v, weights, xs, x_ref, r_ref, u_ref, f_ref, dinv, table, tbuf,
    send, recv, cw, cx, small, big_diag, big_side, fbuf, tw, near_table, inv_s,
    gtile, gather, gfull,
    load_sem, off_sem, send_sem, recv_sem, small_send, small_recv, big_send, big_recv,
    fsend_sem, frecv_sem, gsend_sem, grecv_sem,
):
    nright, nrows, width = f_ref.shape[1], f_ref.shape[0], f_ref.shape[2]
    me = lax.axis_index("dom")
    count = 128
    upper = lax.rem(me + 1, count)
    lower = lax.rem(me + count - 1, count)
    core = lax.rem(me, 2)
    y = lax.rem(me // 2, 4)
    z = lax.rem(me // 8, 4)
    xc = me // 32
    partner = me + 1 - 2 * core

    def member(ax, step):
        if ax == 0:
            return me + 2 * (lax.rem(y + step, 4) - y)
        if ax == 1:
            return me + 8 * (lax.rem(z + step, 4) - z)
        return me + 32 * (lax.rem(xc + step, 4) - xc)

    load_rhs = pltpu.make_async_copy(rhs_hbm, rhs_v, load_sem.at[0])
    load_diag = pltpu.make_async_copy(diag_hbm, diag_v, load_sem.at[1])
    def at_offset(o):
        return lax.rem(me + o + count, count)

    load_inv = [
        pltpu.make_async_copy(
            inv_hbm.at[pl.ds(pl.multiple_of(at_offset(o) * 8, 8), 8)],
            inv_v.at[o + 3], load_sem.at[5 + o],
        )
        for o in range(-3, 4)
    ]
    load_diag.start()
    load_rhs.start()

    def load_off(c):
        rows = pl.ds(c * CHUNK, CHUNK)
        return pltpu.make_async_copy(off_hbm.at[rows], off_v.at[rows], off_sem.at[c])

    for c in range(nrows // CHUNK):
        load_off(c).start()
    for load in load_inv:
        load.start()

    barrier = pltpu.get_barrier_semaphore()
    peers = [at_offset(o) for o in OFFSETS] + [member(ax, s) for ax in range(3) for s in (1, 2, 3)]
    for peer in peers:
        pl.semaphore_signal(barrier, inc=1, device_id=(peer,), device_id_type=MESH)

    wanted = [lists_in[m] for m in range(8)]

    def halo_copies(n, h):
        slot = lax.rem(n, 3)
        half = pl.ds(2 * h, 2)
        up = pltpu.make_async_remote_copy(
            src_ref=send.at[slot, 1, half], dst_ref=recv.at[slot, 0, half],
            send_sem=send_sem.at[slot, 1, h], recv_sem=recv_sem.at[slot, 0, h],
            device_id=(upper,), device_id_type=MESH,
        )
        down = pltpu.make_async_remote_copy(
            src_ref=send.at[slot, 0, half], dst_ref=recv.at[slot, 1, half],
            send_sem=send_sem.at[slot, 0, h], recv_sem=recv_sem.at[slot, 1, h],
            device_id=(lower,), device_id_type=MESH,
        )
        return up, down

    def halo_send(n, value):
        slot = lax.rem(n, 3)
        for h in range(2):
            places = [(side, 2 * h + q) for q in range(2) for side in range(2)]
            values = [value(wanted[4 * side + q]) for side, q in places]
            for (side, q), v in zip(places, values):
                send[slot, side, q] = v
            for copy in halo_copies(n, h):
                copy.start()

    def halo_sent(n):
        for h in range(2):
            for copy in halo_copies(n, h):
                copy.wait_send()

    def halo_take(n):
        slot, par = lax.rem(n, 3), lax.rem(n, 2)
        for h in range(2):
            for copy in halo_copies(n, h):
                copy.wait_recv()
            for q in range(2 * h, 2 * h + 2):
                for side in range(2):
                    xs[par, nrows + 4 * side + q] = split(recv[slot, side, q])

    def product(par, j):
        parts = [xs[par, j]] + [xs[par, cols_in[j * 3 + k]] for k in range(3)]
        res = jnp.dot(
            jnp.concatenate(parts, axis=1), weights[j], preferred_element_type=F32
        )
        return fold(res, nright, width)

    def rows(compute, store):
        def step(g, _):
            values = [compute(g * GROUP + u) for u in range(GROUP)]
            for u in range(GROUP):
                store(g * GROUP + u, values[u])
            return 0

        lax.fori_loop(0, nrows // GROUP, step, 0)

    def publish(par, j, v):
        xs[1 - par, j] = split(v)

    rows_iota = lax.broadcasted_iota(jnp.int32, (width, width), 0)
    eye = rows_iota == lax.broadcasted_iota(jnp.int32, (width, width), 1)
    load_diag.wait()

    def take_diag(i, _):
        d = jnp.sum(jnp.where(eye, diag_v[i], 0.0), axis=0, keepdims=True)
        dinv[i] = 1.0 / d
        return 0

    lax.fori_loop(0, nrows, take_diag, 0)
    load_rhs.wait()
    for i in range(nrows):
        f_ref[i] = rhs_v[:, i * width:(i + 1) * width]

    pl.semaphore_wait(barrier, len(peers))
    halo_send(jnp.int32(0), lambda q: RELAX * dinv[q] * f_ref[q])

    def start_row(j, v):
        x_ref[j] = v
        publish(jnp.int32(1), j, v)

    rows(lambda j: RELAX * dinv[j] * f_ref[j], start_row)

    def big_copies(o):
        return [
            pltpu.make_async_remote_copy(
                src_ref=src, dst_ref=dst.at[3 - o],
                send_sem=big_send.at[i, 3 - o], recv_sem=big_recv.at[i, 3 - o],
                device_id=(at_offset(o),), device_id_type=MESH,
            )
            for i, (src, dst) in enumerate(
                [(cdiag_ref.at[0], big_diag), (cside_ref.at[0], big_side)]
            )
        ]

    for o in OFFSETS[:6]:
        for copy in big_copies(o):
            copy.start()

    def convert(c, _):
        load_off(c).wait()
        for q in range(CHUNK):
            i = c * CHUNK + q
            weights[i, 0:width] = split_columns(diag_v[i].T)
            for k in range(3):
                weights[i, (k + 1) * width:(k + 2) * width] = split_columns(off_v[i, k].T)
        return 0

    lax.fori_loop(0, nrows // CHUNK, convert, 0)

    def make_table(j, sums):
        hot = (agg_ref[j] == rows_iota).astype(F32)
        table[j] = hot.astype(BF16)
        return sums + hot

    sums = lax.fori_loop(0, nrows, make_table, jnp.zeros((width, width), F32))
    count_one = jnp.sum(sums, axis=1, keepdims=True)
    scale_one = (1.0 / jnp.sqrt(jnp.broadcast_to(count_one, (width, width)))).T[0:1]
    hot_two = (cagg_ref[...] == lax.broadcasted_iota(jnp.int32, (8, width), 0)).astype(F32)
    table_two = hot_two * (1.0 / jnp.sqrt(jnp.sum(hot_two, axis=1, keepdims=True)))
    cd = cdiag_ref[0]
    d1inv = 1.0 / jnp.sum(jnp.where(eye, cd, 0.0), axis=0, keepdims=True)
    lists = [agg_ref[wanted[m]].astype(F32) for m in range(8)]
    small[4] = jnp.concatenate(
        [d1inv, scale_one, cagg_ref[...].astype(F32), jnp.zeros((1, width), F32)]
        + lists + [jnp.zeros((4, width), F32)],
        axis=0,
    )

    def small_copy(o):
        return pltpu.make_async_remote_copy(
            src_ref=small.at[4], dst_ref=small.at[4 - o],
            send_sem=small_send.at[4 - o], recv_sem=small_recv.at[4 - o],
            device_id=(at_offset(o),), device_id_type=MESH,
        )

    for o in OFFSETS:
        small_copy(o).start()
    big_diag[3] = cd
    big_side[3] = cside_ref[0]
    for load in load_inv:
        load.wait()
    inv_s[...] = split(jnp.concatenate([inv_v[k] for k in range(7)], axis=0))
    float_rows = rows_iota.astype(F32)

    def take_near():
        for o in OFFSETS[:6]:
            for copy in big_copies(o):
                copy.wait()
        for o in OFFSETS:
            small_copy(o).wait()

        def weigh(k, _):
            cw[k, 0:width] = split_columns(big_diag[k].T)
            cw[k, width:2 * width] = split_columns(big_side[k, 0].T)
            cw[k, 2 * width:3 * width] = split_columns(big_side[k, 1].T)
            shift = (8 * k).astype(F32)
            hot = ((small[k + 1, 2:3] + shift) == float_rows).astype(F32)
            members = jnp.maximum(jnp.sum(hot, axis=1, keepdims=True), 1.0)
            tw[k] = split_columns(hot * (1.0 / jnp.sqrt(members)))
            return 0

        lax.fori_loop(0, 7, weigh, 0)
        for m in range(4):
            near_table[m] = (small[3, 8 + m:9 + m] == float_rows).astype(BF16)
            near_table[4 + m] = (small[5, 4 + m:5 + m] == float_rows).astype(BF16)

    def coarse_copy(cyc, o):
        return pltpu.make_async_remote_copy(
            src_ref=fbuf.at[cyc, 4], dst_ref=fbuf.at[cyc, 4 - o],
            send_sem=fsend_sem.at[cyc, 4 - o], recv_sem=frecv_sem.at[cyc, 4 - o],
            device_id=(at_offset(o),), device_id_type=MESH,
        )

    def coarse_op(o, parts):
        lhs = jnp.concatenate([parts[o], parts[o - 1], parts[o + 1]], axis=1)
        return fold(jnp.dot(lhs, cw[o + 3], preferred_element_type=F32), nright, width)

    chip = me // 2

    def gather_copies(cyc, ax):
        size = (1, 4, 16)[ax]
        first = (chip // size) * size
        out = []
        for s in (1, 2, 3):
            where = gather.at[cyc, pl.ds(first, size)]
            out.append(pltpu.make_async_remote_copy(
                src_ref=where, dst_ref=where,
                send_sem=gsend_sem.at[cyc, ax * 3 + s], recv_sem=grecv_sem.at[cyc, ax * 3 + s],
                device_id=(member(ax, s),), device_id_type=MESH,
            ))
        return out

    def gather_waits(cyc, ax):
        size = (1, 4, 16)[ax]
        for s in (1, 2, 3):
            source = member(ax, 4 - s) // 2
            where = gather.at[cyc, pl.ds((source // size) * size, size)]
            pltpu.make_async_remote_copy(
                src_ref=where, dst_ref=where,
                send_sem=gsend_sem.at[cyc, ax * 3 + s], recv_sem=grecv_sem.at[cyc, ax * 3 + s],
                device_id=(member(ax, s),), device_id_type=MESH,
            ).wait_recv()

    def gather_all(cyc, tile, between):
        gtile[cyc, 0] = tile
        pair = pltpu.make_async_remote_copy(
            src_ref=gtile.at[cyc, 0], dst_ref=gtile.at[cyc, 1],
            send_sem=gsend_sem.at[cyc, 0], recv_sem=grecv_sem.at[cyc, 0],
            device_id=(partner,), device_id_type=MESH,
        )
        pair.start()
        pair.wait()
        other = gtile[cyc, 1]
        even = jnp.where(core == 0, tile, other)
        odd = jnp.where(core == 0, other, tile)
        low_lanes = lax.broadcasted_iota(jnp.int32, (8, width), 1) < nright
        gather[cyc, pl.ds(chip, 1)] = jnp.where(low_lanes, even, pltpu.roll(odd, nright, 1))[None]
        for ax in range(3):
            copies = gather_copies(cyc, ax)
            for copy in copies:
                copy.start()
            gather_waits(cyc, ax)
            for copy in copies:
                copy.wait_send()
            if ax == 0:
                between()
        for c in range(64):
            pair_tile = gather[cyc, c]
            gfull[16 * c:16 * c + 8] = split_columns(pair_tile)
            gfull[16 * c + 8:16 * c + 16] = split_columns(pltpu.roll(pair_tile, nright, 1))

    def sweep(n, last):
        par = lax.rem(n, 2)
        halo_take(n)

        def relax(j):
            d = RELAX * dinv[j]
            return x_ref[j] + d * (f_ref[j] - product(par, j))

        def body(j, new):
            x_ref[j] = new
            publish(par, j, new)

        if last is None:
            halo_send(n + 1, relax)
        else:
            @pl.when(n < last)
            def _():
                halo_send(n + 1, relax)
        rows(relax, body)
        if last is None:
            halo_sent(n + 1)
        else:
            @pl.when(n < last)
            def _():
                halo_sent(n + 1)

    halo_sent(jnp.int32(0))
    sweep(jnp.int32(0), None)
    take_near()

    def cycle(cyc, _):
        n = 1 + 7 * cyc
        par = lax.rem(n, 2)
        halo_take(n)

        def resid(j):
            return f_ref[j] - product(par, j)

        def resid_row(j, r):
            r_ref[j] = r
            publish(par, j, dinv[j] * r)

        halo_send(n + 1, lambda q: dinv[q] * resid(q))
        rows(resid, resid_row)
        halo_sent(n + 1)

        n1 = n + 1
        par1 = lax.rem(n1, 2)
        halo_take(n1)

        def smooth(j):
            return r_ref[j] - SMOOTH * product(par1, j)

        def smooth_row(j, t):
            tbuf[j] = split(t)

        rows(smooth, smooth_row)

        def restrict(g, acc):
            for u in range(8):
                j = g * 8 + u
                acc = acc + lax.dot_general(
                    tbuf[j], table[j], (((1,), (1,)), ((), ())), preferred_element_type=F32
                )
            return acc

        acc = lax.fori_loop(0, nrows // 8, restrict, jnp.zeros((2 * nright, width), F32))
        right_one = (acc[:nright] + acc[nright:]) * scale_one

        fbuf[cyc, 4] = right_one
        for o in OFFSETS[:4]:
            coarse_copy(cyc, o).start()
        rate = {o: RELAX * small[o + 4, 0:1] for o in range(-4, 5)}
        rhs_one, it, parts = {}, {}, {}

        def first(o):
            rhs_one[o] = fbuf[cyc, o + 4]
            it[o] = rate[o] * rhs_one[o]
            parts[o] = split(it[o])

        def improve(offsets):
            return {
                o: it[o] + rate[o] * (rhs_one[o] - coarse_op(o, parts)) for o in offsets
            }

        first(0)
        for o in OFFSETS[:4]:
            coarse_copy(cyc, -o).wait_recv()
            first(o)
        second = improve((-1, 0, 1))
        resid_one = rhs_one[0] - coarse_op(0, {o: split(second[o]) for o in second})
        padded = jnp.concatenate([resid_one, jnp.zeros((width - nright, width), F32)], axis=0)
        tile = lax.dot_general(
            table_two, padded, (((1,), (1,)), ((), ())),
            precision=lax.Precision.HIGHEST, preferred_element_type=F32,
        )

        def send_far():
            for o in OFFSETS[4:]:
                coarse_copy(cyc, o).start()

        gather_all(cyc, tile, send_far)
        e2 = fold(jnp.dot(inv_s[...], gfull[...], preferred_element_type=F32), 56, width)
        e2t = split(
            jnp.concatenate([e2, jnp.zeros((width - 56, width), F32)], axis=0).T[:nright]
        )
        for o in OFFSETS[4:]:
            coarse_copy(cyc, -o).wait_recv()
            first(o)
        second.update(improve((-3, -2, 2, 3)))
        it = {
            o: second[o]
            + fold(jnp.dot(e2t, tw[o + 3], preferred_element_type=F32), nright, width)
            for o in second
        }
        parts = {o: split(it[o]) for o in it}
        it = improve((-2, -1, 0, 1, 2))
        parts = {o: split(it[o]) for o in it}
        it = improve((-1, 0, 1))
        for o in (-1, 0, 1):
            cx[o + 1] = split(it[o] * small[o + 4, 1:2])
        for o in OFFSETS:
            coarse_copy(cyc, o).wait_send()

        n2 = n + 2
        par2 = lax.rem(n2, 2)

        def lifted(value, hot):
            res = jnp.dot(value, hot, preferred_element_type=F32)
            return res[:nright] + res[nright:]

        def lift(j):
            return lifted(cx[1], table[j])

        def lift_row(j, u):
            u_ref[j] = u
            publish(1 - par2, j, u)

        rows(lift, lift_row)
        for m in range(8):
            xs[par2, nrows + m] = split(lifted(cx[2 * (m // 4)], near_table[m]))

        def correct(j):
            d = SMOOTH * dinv[j]
            return x_ref[j] + u_ref[j] - d * product(par2, j)

        def correct_row(j, new):
            x_ref[j] = new
            publish(par2, j, new)

        halo_send(n2 + 1, correct)
        rows(correct, correct_row)
        halo_sent(n2 + 1)

        def sweeps(s, _):
            sweep(n2 + 1 + s, 12)
            return 0

        lax.fori_loop(0, 4 - 2 * cyc, sweeps, 0)
        return 0

    lax.fori_loop(0, 2, cycle, 0)
    for i in range(nrows):
        out_ref[:, i * width:(i + 1) * width] = x_ref[i]


def local(
    rhs_fields, diag_blocks, off_blocks, block_cols, send_lists, fine_agg,
    coarse_diag, coarse_side, coarse_agg, coarse_inverse,
):
    nrows, width = diag_blocks.shape[0], diag_blocks.shape[1]
    nright = rhs_fields.shape[0]
    naggs = coarse_diag.shape[1]
    S = pl.BlockSpec(memory_space=pltpu.SMEM)
    V = pl.BlockSpec(memory_space=pltpu.VMEM)
    A = pl.BlockSpec(memory_space=pl.ANY)
    DMA = pltpu.SemaphoreType.DMA
    return pl.pallas_call(
        kernel,
        name="multigrid",
        out_shape=jax.ShapeDtypeStruct(rhs_fields.shape, F32),
        in_specs=[S, S, A, A, A, V, V, V, V, A],
        out_specs=V,
        scratch_shapes=[
            pltpu.VMEM(rhs_fields.shape, F32),
            pltpu.VMEM(diag_blocks.shape, F32),
            pltpu.VMEM(off_blocks.shape, F32),
            pltpu.VMEM((7, 8, coarse_inverse.shape[1]), F32),
            pltpu.VMEM((nrows, 4 * width, 2 * width), BF16),
            pltpu.VMEM((2, nrows + 8, 2 * nright, width), BF16),
            pltpu.VMEM((nrows, nright, width), F32),
            pltpu.VMEM((nrows, nright, width), F32),
            pltpu.VMEM((nrows, nright, width), F32),
            pltpu.VMEM((nrows, nright, width), F32),
            pltpu.VMEM((nrows, 1, width), F32),
            pltpu.VMEM((nrows, naggs, width), BF16),
            pltpu.VMEM((nrows, 2 * nright, width), BF16),
            pltpu.VMEM((3, 2, 4, nright, width), F32),
            pltpu.VMEM((3, 2, 4, nright, width), F32),
            pltpu.VMEM((7, 3 * width, 2 * width), BF16),
            pltpu.VMEM((3, 2 * nright, width), BF16),
            pltpu.VMEM((9, 16, width), F32),
            pltpu.VMEM((7, width, width), F32),
            pltpu.VMEM((7, 2, width, width), F32),
            pltpu.VMEM((2, 9, nright, width), F32),
            pltpu.VMEM((7, width, 2 * width), BF16),
            pltpu.VMEM((8, width, width), BF16),
            pltpu.VMEM((112, coarse_inverse.shape[1]), BF16),
            pltpu.VMEM((2, 2, 8, width), F32),
            pltpu.VMEM((2, 64, 8, width), F32),
            pltpu.VMEM((1024, 2 * width), BF16),
            DMA((9,)),
            DMA((nrows // CHUNK,)),
            DMA((3, 2, 2)),
            DMA((3, 2, 2)),
            DMA((9,)),
            DMA((9,)),
            DMA((2, 7)),
            DMA((2, 7)),
            DMA((2, 9)),
            DMA((2, 9)),
            DMA((2, 10)),
            DMA((2, 10)),
        ],
        compiler_params=pltpu.CompilerParams(
            collective_id=0, has_side_effects=True, vmem_limit_bytes=60 * 1024 * 1024
        ),
    )(
        block_cols.reshape(-1), send_lists.reshape(-1),
        rhs_fields, diag_blocks, off_blocks, fine_agg.reshape(nrows, 1, width),
        coarse_diag, coarse_side, coarse_agg.reshape(1, naggs), coarse_inverse,
    )


def solution(mesh):
    return jax.shard_map(
        local,
        mesh=mesh,
        in_specs=(
            P(None, "dom"),
            P("dom", None, None),
            P("dom", None, None, None),
            P("dom", None),
            P("dom", None, None),
            P("dom"),
            P("dom", None, None),
            P("dom", None, None, None),
            P("dom"),
            P(),
        ),
        out_specs=P(None, "dom"),
        check_vma=False,
    )
```
